32 devices in a mesh: groups: 2 (over x), ctx: 4 (over y, core), heads: 4 (over z).
Axes of the slice: x: 2, y: 2, z: 4, core: 2. Of those that a mesh axis runs over, the one named last changes fastest.
Arguments:
- tokens: bfloat16 [4096, 2048], P(('groups', 'ctx', 'heads')), parts along dimension 0, may hold values from -60 to 60
- state_in: float32 [4, 256, 128], P('heads', 'groups'), parts along dimension 1, may hold values from -256 to 256
- past_kv: bfloat16 [2, 1024, 512], P(None, 'groups', 'heads'), parts along dimension 1, may hold values from -6 to 6
- w_qkv: bfloat16 [2048, 3, 512], P(None, None, 'heads'), may hold values from -0.125 to 0.125
- w_out: bfloat16 [512, 2048], P('heads'), may hold values from -0.25 to 0.25
- w_gate: bfloat16 [16, 2048, 768], P(('ctx', 'heads')), may hold values from -0.125 to 0.125
- w_up: bfloat16 [16, 2048, 768], P(('ctx', 'heads')), may hold values from -0.125 to 0.125
- w_down: bfloat16 [16, 768, 2048], P(('ctx', 'heads')), may hold values from -0.21875 to 0.21875
- expert_ids: int32 [4096, 8], P(('groups', 'ctx', 'heads')), parts along dimension 0, may hold values from 0 to 15, all different within a row; in each aligned block of 128 rows (0 to 127, 128 to 255, ...) at most 128 rows name the same one
- gate_weights: float32 [4096, 8], P(('groups', 'ctx', 'heads')), parts along dimension 0, may hold values from 0.1 to 1
Outputs:
- mixed: bfloat16 [4096, 2048], P(('groups', 'ctx', 'heads')), parts along dimension 0
The draws below stay inside these ranges and needn't reach their ends.
There are 2 independent parts, one for each index of `groups`. The reference program is written for one: setup_inputs(seed, part) draws one part's arguments, and reference() takes and returns one part's arrays. A program takes and returns all parts, laid end to end along the dimension named above; an argument that names none is the same for every part. Nothing has to cross between parts.
Inputs may be any that keep to these rules, and one draw needn't show every extreme that they name: `expert_ids`: each row names 8 different experts; in each aligned block of 128 rows (the rows of one device) no expert is named by more than 128 rows, a bound that some block reaches.
All inputs are finite; a program needn't handle non-finite values.
Results may differ from the reference program's by a relative error of at most 0.017.
Values may be sent and summed in bfloat16 or wider, within the bound.
A program may use at most 128 MiB of HBM per device.

```python
import math
import jax
import jax.numpy as jnp
import numpy as np
from jax import lax

D = 2048
HDIM = 128
INNER = 768
TOP = 8
WINDOW = 512
TOK_DEV = 512
TOKENS = 2048
ROWS = 128
HEADS = 4
EXPERTS = 16
CAP = 128


def draw_tokens(key, part):
    base_key = jax.random.fold_in(jax.random.fold_in(key, 11), 0)
    values = jax.random.normal(base_key, (TOKENS, D), jnp.float32)
    return jnp.clip(values, -60.0, 60.0).astype(jnp.bfloat16)


def block_scale(stream_key, dims, shards, low, largest):
    def one(axis_at, parts):
        draws = jax.random.uniform(jax.random.fold_in(jax.random.fold_in(stream_key, 6), axis_at), (parts,), jnp.float32, low / len(shards), largest / len(shards))
        return jnp.repeat(jnp.exp(draws), dims[axis_at] // parts).reshape((-1,) + (1,) * (len(dims) - axis_at - 1))

    gain = one(*shards[0])
    for cut in shards[1:]:
        gain = gain * one(*cut)
    return gain


def routed_block(key, own, number, rows, amount, top, most, slope):
    sequence = jax.random.permutation(key, amount)
    crowded, common = shares(amount, rows * top, most, slope, True), shares(amount, rows * top, most, slope, False)
    places = jnp.arange(amount)

    def named(tallies, offset_by):
        used = int((tallies > 0).sum())
        fixed = max(1, used // 4)
        shifted = fixed + (places - fixed + offset_by * (used - fixed)) % max(1, amount - fixed)
        return jnp.zeros((amount,), jnp.int32).at[sequence[jnp.where(places < fixed, places, shifted)]].set(jnp.asarray(tallies, jnp.int32))

    tallies = jnp.where(number % 4 == 0, named(crowded, number // 4), named(common, number - number // 4 - 1))
    mixed = jax.random.permutation(jax.random.fold_in(own, 3), amount)
    source_of, taker = mixed[0:amount // 2 * 2:2], mixed[1:amount // 2 * 2:2]
    room = jnp.minimum(tallies[source_of] - 1, most - tallies[taker]) // 2
    room = jnp.where((source_of == sequence[0]) | (taker == sequence[0]) | (tallies[taker] == 0), 0, jnp.maximum(room, 0))
    shifted = jax.random.randint(jax.random.fold_in(own, 4), (amount // 2,), 0, 1 << 20) % (room + 1)
    tallies = tallies.at[source_of].add(-shifted).at[taker].add(shifted)
    labels = jnp.searchsorted(jnp.cumsum(tallies), jnp.arange(rows * top), side="right").astype(jnp.int32)
    grid = labels.reshape(top, rows).T
    grid = grid[jax.random.permutation(jax.random.fold_in(own, 1), rows)]
    offset_by = jax.random.randint(jax.random.fold_in(own, 2), (rows, 1), 0, top)
    return jnp.take_along_axis(grid, (jnp.arange(top)[None, :] + offset_by) % top, axis=1)


def shares(number_of, total, limit, slope, full):
    portions = [(1 << 20) // math.isqrt(grade ** slope) + 1 for grade in range(1, number_of + 1)]
    largest = limit if full else min(limit, max(-(-total // number_of), total * portions[0] // sum(portions)))
    least = 1 if total - largest >= number_of - 1 else 0
    given, rest = [largest] + [least] * (number_of - 1), total - largest - least * (number_of - 1)
    while rest > 0:
        candidates = [i for i in range(1, number_of) if given[i] < largest] or [i for i in range(1, number_of) if given[i] < limit]
        whole, left = sum([portions[i] for i in candidates]), rest
        for i in candidates:
            more = min(limit - given[i], max(1, left * portions[i] // whole), rest)
            given[i] = given[i] + more
            rest = rest - more
    return np.array(given)


def normal_values(stream_key, dims, scale, bound, cuts=(), kind=jnp.bfloat16):
    result = scale * jax.random.normal(stream_key, dims, jnp.float32)
    if cuts:
        result = result * block_scale(stream_key, dims, cuts, -0.22, 0.18)
    return jnp.clip(result, -bound, bound).astype(kind)


def setup_inputs(seed: int = 0, part: int = 0) -> dict:
    splits = jax.random.split(jax.random.key(seed), 11)
    own_keys = jax.random.split(jax.random.fold_in(splits[10], part), 11)
    tokens = draw_tokens(jax.random.fold_in(jax.random.fold_in(splits[10], part), 71), part)
    state_in = normal_values(own_keys[1], (HEADS, HDIM, HDIM), (TOKENS ** 0.5), 256.0, ((0, 4),), jnp.float32)
    past_kv = normal_values(own_keys[2], (2, WINDOW, HEADS * HDIM), 1.0, 6.0, ((2, 4),))
    w_qkv = normal_values(splits[3], (D, 3, HEADS * HDIM), D ** -0.5, 0.125, ((2, 4),))
    w_out = normal_values(splits[4], (HEADS * HDIM, D), (HEADS * HDIM) ** -0.5, 0.25, ((0, 4),))
    w_gate = normal_values(splits[5], (EXPERTS, D, INNER), D ** -0.5, 0.125, ((0, 16),))
    w_up = normal_values(splits[6], (EXPERTS, D, INNER), D ** -0.5, 0.125, ((0, 16),))
    w_down = normal_values(splits[7], (EXPERTS, INNER, D), INNER ** -0.5, 0.21875, ((0, 16),))
    expert_ids_keys = jax.random.split(jax.random.fold_in(own_keys[8], 1), TOKENS // ROWS)
    expert_ids_turns = jax.random.permutation(jax.random.fold_in(own_keys[8], 3), TOKENS // ROWS)
    expert_ids = jax.vmap(lambda own, number: routed_block(jax.random.fold_in(own_keys[8], 2), own, number, ROWS, EXPERTS, TOP, CAP, 2))(expert_ids_keys, expert_ids_turns).reshape((TOKENS, TOP))
    gate_weights = jnp.clip(jnp.exp(math.log(1.0) - 2.3025851 * jax.random.uniform(own_keys[9], (TOKENS, TOP), jnp.float32) ** block_scale(own_keys[9], (TOKENS, TOP), ((0, 16),), -0.2, 0.2)), 0.1, 1.0)
    return dict(tokens=tokens, state_in=state_in, past_kv=past_kv, w_qkv=w_qkv, w_out=w_out, w_gate=w_gate, w_up=w_up, w_down=w_down, expert_ids=expert_ids, gate_weights=gate_weights)


def normalize(value):
    return value * lax.rsqrt(lax.optimization_barrier(jnp.mean(value * value, axis=-1, keepdims=True)) + 1e-06)

def one_head(query, keys, values, start_state, past_keys, past_values):
    block_rows = min(TOK_DEV, 512)
    block_count = TOKENS // block_rows
    scale = 1.0 / math.sqrt(HDIM)
    causal = jnp.arange(block_rows)[:, None] >= jnp.arange(block_rows)[None, :]
    offsets = jnp.arange(WINDOW + block_rows)[None, :] - jnp.arange(block_rows)[:, None]
    in_window = (offsets > 0) & (offsets <= WINDOW)
    all_keys = jnp.concatenate([past_keys, keys], axis=0)
    all_values = jnp.concatenate([past_values, values], axis=0)

    def step(state, index):
        first = (index * block_rows).astype(jnp.int32)
        q_block = lax.dynamic_slice_in_dim(query, first, block_rows, 0)
        k_block = lax.dynamic_slice_in_dim(keys, first, block_rows, 0)
        v_block = lax.dynamic_slice_in_dim(values, first, block_rows, 0)
        carried = jnp.dot(q_block.astype(jnp.float32), state, precision=lax.Precision.HIGHEST)
        inside = jnp.dot(q_block, k_block.T, preferred_element_type=jnp.float32)
        inside = jnp.where(causal, inside, 0.0).astype(jnp.bfloat16)
        linear = carried + jnp.dot(inside, v_block, preferred_element_type=jnp.float32)
        w_keys = lax.dynamic_slice_in_dim(all_keys, first, WINDOW + block_rows, 0)
        w_values = lax.dynamic_slice_in_dim(all_values, first, WINDOW + block_rows, 0)
        scores = jnp.dot(q_block, w_keys.T, preferred_element_type=jnp.float32) * scale
        scores = jnp.where(in_window, scores, -jnp.inf)
        top_score = lax.optimization_barrier(jnp.max(scores, axis=-1, keepdims=True))
        expo = jnp.exp(scores - top_score)
        probs = (expo / lax.optimization_barrier(jnp.sum(expo, axis=-1, keepdims=True))).astype(jnp.bfloat16)
        window_out = jnp.dot(probs, w_values, preferred_element_type=jnp.float32)
        combined = (normalize(linear) + window_out).astype(jnp.bfloat16)
        new_state = state + jnp.dot(k_block.T, v_block, preferred_element_type=jnp.float32)
        return (new_state, combined)
    _, outs = lax.scan(step, start_state, jnp.arange(block_count, dtype=jnp.int32))
    return outs.reshape(TOKENS, HDIM)

def slot_block(block_ids):
    onehot = (block_ids[:, None] == jnp.arange(EXPERTS, dtype=jnp.int32)[None, :]).astype(jnp.int32)
    earlier = jnp.cumsum(onehot, axis=0) - onehot
    return lax.optimization_barrier(jnp.sum(onehot * earlier, axis=1)).astype(jnp.int32)

def reference(tokens, state_in, past_kv, w_qkv, w_out, w_gate, w_up, w_down, expert_ids, gate_weights):
    projected = jnp.dot(tokens, w_qkv.reshape(D, 3 * HEADS * HDIM), preferred_element_type=jnp.float32)
    projected = projected.astype(jnp.bfloat16).reshape(TOKENS, 3, HEADS, HDIM)
    query = jnp.transpose(projected[:, 0], (1, 0, 2))
    keys = jnp.transpose(projected[:, 1], (1, 0, 2))
    values = jnp.transpose(projected[:, 2], (1, 0, 2))
    past = jnp.transpose(past_kv.reshape(2, WINDOW, HEADS, HDIM), (0, 2, 1, 3))

    def per_head(inputs):
        return one_head(*inputs)
    heads_out = lax.map(per_head, (query, keys, values, state_in, past[0], past[1]))
    heads_out = jnp.transpose(heads_out, (1, 0, 2)).reshape(TOKENS, HEADS * HDIM)
    attn = jnp.dot(heads_out, w_out, preferred_element_type=jnp.float32)
    hidden_state = (tokens.astype(jnp.float32) + attn).astype(jnp.bfloat16)
    normed = normalize(hidden_state.astype(jnp.float32)).astype(jnp.bfloat16)
    sources = TOKENS // ROWS
    picks = expert_ids.reshape(sources, ROWS * TOP).astype(jnp.int32)
    slots = lax.map(slot_block, picks)
    source_ids = jnp.broadcast_to(jnp.arange(sources, dtype=jnp.int32)[:, None], picks.shape)
    token_ids = source_ids * ROWS + (jnp.arange(ROWS * TOP, dtype=jnp.int32) // TOP)[None, :]
    table = jnp.full((EXPERTS, sources, CAP), TOKENS, jnp.int32).at[picks, source_ids, slots].set(token_ids)
    weight_table = jnp.zeros((EXPERTS, sources, CAP), jnp.float32).at[picks, source_ids, slots].set(gate_weights.reshape(sources, ROWS * TOP))
    padded = jnp.concatenate([normed, jnp.zeros((1, D), jnp.bfloat16)], axis=0)

    def expert_step(total, inputs):
        index_rows, weight_rows, gate_mat, up_mat, down_mat = inputs
        flat_index = index_rows.reshape(-1)
        rows_in = padded[flat_index]
        gate_act = jnp.dot(rows_in, gate_mat, preferred_element_type=jnp.float32)
        up_act = jnp.dot(rows_in, up_mat, preferred_element_type=jnp.float32)
        hid = (jax.nn.silu(gate_act) * up_act).astype(jnp.bfloat16)
        out_rows = jnp.dot(hid, down_mat, preferred_element_type=jnp.float32).astype(jnp.bfloat16)
        total = total.at[flat_index].add(weight_rows.reshape(-1)[:, None] * out_rows.astype(jnp.float32))
        return (total, None)
    total, _ = lax.scan(expert_step, jnp.zeros((TOKENS + 1, D), jnp.float32), (table, weight_table, w_gate, w_up, w_down))
    return (hidden_state.astype(jnp.float32) + total[:TOKENS]).astype(jnp.bfloat16)
```

```python
import math

import jax
import jax.numpy as jnp
from jax import lax
from jax.sharding import PartitionSpec as P

HDIM = 128
WINDOW = 512


def entering(x, axis, join, neutral):
    place = lax.axis_index(axis)
    gathered = lax.all_gather(x.astype(jnp.bfloat16), axis)
    state = jnp.zeros_like(x) + jnp.asarray(neutral, x.dtype)

    def one(lap, state):
        return join(state, lax.dynamic_index_in_dim(gathered, lap, 0, False).astype(x.dtype))

    return lax.fori_loop(0, place, one, state)


def from_behind(block, axis, distance):
    devices = range(lax.axis_size(axis))
    route = [(i - distance, i) for i in devices if i - distance in devices]
    return lax.ppermute(block, axis, route)


def normalize(value):
    return value * lax.rsqrt(jnp.mean(value * value, axis=-1, keepdims=True) + 1e-06)


def dense_experts(
    hidden_float, normed, w_gate, w_up, w_down, expert_ids, gate_weights, expert_count
):
    axes = ("ctx", "heads")
    exp_local = w_gate.shape[0]
    chosen = expert_ids[:, :, None] == jnp.arange(expert_count, dtype=jnp.int32)
    table = jnp.sum(jnp.where(chosen, gate_weights[:, :, None], 0.0), axis=1)
    weights = lax.all_gather(table, axes, axis=0, tiled=True)
    first = lax.axis_index(axes) * exp_local
    rows = lax.all_gather(normed, axes, axis=0, tiled=True)
    total = None
    for e in range(exp_local):
        gate_act = jnp.dot(rows, w_gate[e], preferred_element_type=jnp.float32)
        up_act = jnp.dot(rows, w_up[e], preferred_element_type=jnp.float32)
        hid = (jax.nn.silu(gate_act) * up_act).astype(jnp.bfloat16)
        out_rows = jnp.dot(hid, w_down[e], preferred_element_type=jnp.float32)
        weight = lax.dynamic_slice_in_dim(weights, first + e, 1, 1)
        part = weight * out_rows
        total = part if total is None else total + part
    routed = lax.psum_scatter(
        total.astype(jnp.bfloat16), axes, scatter_dimension=0, tiled=True
    )
    return (hidden_float + routed.astype(jnp.float32)).astype(jnp.bfloat16)


def on_device(
    tokens, state_in, past_kv, w_qkv, w_out, w_gate, w_up, w_down, expert_ids, gate_weights
):
    row_count, model_width = tokens.shape
    inner_width = w_qkv.shape[2]
    local_heads = inner_width // HDIM
    w_flat = w_qkv.reshape(model_width, 3 * inner_width)
    projected = jnp.dot(
        lax.all_gather(tokens, "heads", axis=0, tiled=True),
        w_flat,
        preferred_element_type=jnp.float32,
    ).astype(jnp.bfloat16)
    slab_rows = projected.shape[0]
    projected = projected.reshape(slab_rows, 3, local_heads, HDIM)
    query = jnp.transpose(projected[:, 0], (1, 0, 2))
    keys = jnp.transpose(projected[:, 1], (1, 0, 2))
    values = jnp.transpose(projected[:, 2], (1, 0, 2))
    local_state = jnp.einsum("hsd,hse->hde", keys, values, preferred_element_type=jnp.float32)
    earlier_state = entering(
        local_state, "ctx", lambda first, second: first + second, jnp.zeros_like(local_state)
    )
    start_state = state_in + earlier_state
    tail = jnp.stack([keys, values], axis=0)
    arrived = from_behind(tail, "ctx", 1)
    past = jnp.transpose(past_kv.reshape(2, WINDOW, local_heads, HDIM), (0, 2, 1, 3))
    previous = jnp.where(lax.axis_index("ctx") == 0, past, arrived)
    all_keys = jnp.concatenate([previous[0], keys], axis=1)
    all_values = jnp.concatenate([previous[1], values], axis=1)
    block_rows = min(slab_rows, 512)
    block_count = slab_rows // block_rows
    scale = 1.0 / math.sqrt(HDIM)
    causal = jnp.arange(block_rows)[:, None] >= jnp.arange(block_rows)[None, :]
    offsets = jnp.arange(WINDOW + block_rows)[None, :] - jnp.arange(block_rows)[:, None]
    in_window = (offsets > 0) & (offsets <= WINDOW)

    def block_step(state, index):
        first = index * block_rows
        carried = jnp.einsum(
            "hsd,hde->hse", query.astype(jnp.float32), state, precision=lax.Precision.HIGHEST
        )
        inside = jnp.einsum("hsd,htd->hst", query, keys, preferred_element_type=jnp.float32)
        inside = jnp.where(causal[None], inside, 0.0).astype(jnp.bfloat16)
        linear = carried + jnp.einsum(
            "hst,hte->hse", inside, values, preferred_element_type=jnp.float32
        )
        scores = (
            jnp.einsum("hsd,htd->hst", query, all_keys, preferred_element_type=jnp.float32) * scale
        )
        scores = jnp.where(in_window[None], scores, -jnp.inf)
        top_score = jnp.max(scores, axis=-1, keepdims=True)
        expo = jnp.exp(scores - top_score)
        probs = (expo / jnp.sum(expo, axis=-1, keepdims=True)).astype(jnp.bfloat16)
        window_out = jnp.einsum(
            "hst,hte->hse", probs, all_values, preferred_element_type=jnp.float32
        )
        combined = (normalize(linear) + window_out).astype(jnp.bfloat16)
        new_state = state + jnp.einsum(
            "hsd,hse->hde", keys, values, preferred_element_type=jnp.float32
        )
        return (new_state, combined)

    _, outs = lax.scan(block_step, start_state, jnp.arange(block_count, dtype=jnp.int32))
    heads_out = jnp.transpose(outs, (0, 2, 1, 3)).reshape(slab_rows, inner_width)
    regrouped = lax.all_to_all(heads_out, "heads", split_axis=0, concat_axis=1, tiled=True)
    attn = jnp.dot(
        regrouped,
        lax.all_gather(w_out, "heads", axis=0, tiled=True),
        preferred_element_type=jnp.float32,
    )
    hidden_state = (tokens.astype(jnp.float32) + attn).astype(jnp.bfloat16)
    hidden_float = hidden_state.astype(jnp.float32)
    normed = normalize(hidden_float).astype(jnp.bfloat16)
    ctx_count = lax.axis_size("ctx")
    head_count = lax.axis_size("heads")
    exp_local = w_gate.shape[0]
    expert_count = exp_local * ctx_count * head_count
    top_count = expert_ids.shape[1]
    capacity = max(2, 2 * row_count * top_count // expert_count)
    devices = ctx_count * head_count
    if row_count * devices <= expert_count * capacity:
        return dense_experts(
            hidden_float, normed, w_gate, w_up, w_down, expert_ids, gate_weights, expert_count
        )
    picks = expert_ids.reshape(-1)
    onehot = (picks[:, None] == jnp.arange(expert_count, dtype=jnp.int32)[None, :]).astype(
        jnp.int32
    )
    earlier = jnp.cumsum(onehot, axis=0) - onehot
    slots = jnp.sum(onehot * earlier, axis=1)
    destination = picks * capacity + slots
    source_rows = jnp.arange(row_count * top_count, dtype=jnp.int32) // top_count
    outgoing = jnp.zeros((expert_count * capacity, model_width), jnp.bfloat16)
    outgoing = outgoing.at[destination].set(normed[source_rows])
    sendable = outgoing.reshape(expert_count, 1, capacity, model_width)
    arrived_rows = lax.all_to_all(
        sendable, ("ctx", "heads"), split_axis=0, concat_axis=1, tiled=True
    )
    e_count, n_count, c_count, d_count = arrived_rows.shape
    flat = arrived_rows.reshape(e_count, n_count * c_count, d_count)
    gate_act = jnp.einsum("erd,edf->erf", flat, w_gate, preferred_element_type=jnp.float32)
    up_act = jnp.einsum("erd,edf->erf", flat, w_up, preferred_element_type=jnp.float32)
    hid = (jax.nn.silu(gate_act) * up_act).astype(jnp.bfloat16)
    out_rows = jnp.einsum("erf,efd->erd", hid, w_down, preferred_element_type=jnp.float32)
    finished = out_rows.astype(jnp.bfloat16).reshape(e_count, n_count, c_count, d_count)
    returned = lax.all_to_all(finished, ("ctx", "heads"), split_axis=1, concat_axis=0, tiled=True)
    returned = returned.reshape(expert_count * capacity, model_width)
    picked = returned[destination].reshape(row_count, top_count, model_width).astype(jnp.float32)
    routed = jnp.sum(gate_weights[:, :, None] * picked, axis=1)
    return (hidden_float + routed).astype(jnp.bfloat16)


def solution(mesh):
    return jax.shard_map(
        on_device,
        mesh=mesh,
        in_specs=(
            P(("groups", "ctx", "heads"), None),
            P("heads", "groups", None),
            P(None, "groups", "heads"),
            P(None, None, "heads"),
            P("heads", None),
            P(("ctx", "heads"), None, None),
            P(("ctx", "heads"), None, None),
            P(("ctx", "heads"), None, None),
            P(("groups", "ctx", "heads"), None),
            P(("groups", "ctx", "heads"), None),
        ),
        out_specs=P(("groups", "ctx", "heads"), None),
        check_vma=False,
    )
```

```python
import functools
import math

import jax
import jax.numpy as jnp
from jax import lax
from jax.experimental import pallas as pl
from jax.experimental.pallas import tpu as pltpu
from jax.sharding import PartitionSpec as P

HDIM = 128
WINDOW = 512


def entering(x, axis, join, neutral):
    place = lax.axis_index(axis)
    gathered = lax.all_gather(x.astype(jnp.bfloat16), axis)
    state = jnp.zeros_like(x) + jnp.asarray(neutral, x.dtype)

    def one(lap, state):
        return join(state, lax.dynamic_index_in_dim(gathered, lap, 0, False).astype(x.dtype))

    return lax.fori_loop(0, place, one, state)


def from_behind(block, axis, distance):
    devices = range(lax.axis_size(axis))
    route = [(i - distance, i) for i in devices if i - distance in devices]
    return lax.ppermute(block, axis, route)


def normalize(value):
    return value * lax.rsqrt(jnp.mean(value * value, axis=-1, keepdims=True) + 1e-06)


MESH = pl.DeviceIdType.MESH
VMEM_BYTES = 60 * 1024 * 1024
ADD_ROWS = 16


def place(count):
    z = lax.axis_index("heads")
    c = lax.axis_index("ctx")
    beside = c + 1 - 2 * lax.rem(c, 2)
    across = lax.rem(c + 2, 4)
    diagonal = lax.rem(beside + 2, 4)
    return z, c, beside, across, diagonal


def greet(z, count, beside, across):
    barrier = pltpu.get_barrier_semaphore()

    def signal(target):
        pl.semaphore_signal(barrier, inc=1, device_id=target, device_id_type=MESH)

    signal({"ctx": beside})
    signal({"ctx": across})

    @pl.when(z > 0)
    def _():
        signal({"heads": z - 1})

    @pl.when(z < count - 1)
    def _():
        signal({"heads": z + 1})

    pl.semaphore_wait(barrier, 2 + jnp.minimum(z, 1) + jnp.minimum(count - 1 - z, 1))


def gather_kernel(
    count, x_ref, t_ref, rows_ref, table_ref, send_x, send_t, recv_x, recv_t, own_sem
):
    z, c, beside, across, diagonal = place(count)
    greet(z, count, beside, across)

    def copies(zz, cc, way, target, own=False):
        slot = cc * count + zz
        return [
            pltpu.make_async_remote_copy(
                src_ref=source if own else full.at[slot],
                dst_ref=full.at[slot],
                send_sem=send.at[way, slot],
                recv_sem=recv.at[slot],
                device_id=target,
                device_id_type=MESH,
            )
            for source, full, send, recv in (
                (x_ref, rows_ref, send_x, recv_x),
                (t_ref, table_ref, send_t, recv_t),
            )
        ]

    def start(zz, cc, way, target, own=False):
        for copy in copies(zz, cc, way, target, own):
            copy.start()

    def arrived(zz, cc):
        for copy in copies(zz, cc, 0, {"ctx": beside}):
            copy.wait_recv()

    def left(zz, cc, way, target):
        for copy in copies(zz, cc, way, target):
            copy.wait_send()

    def along(act, down, up, zz, **options):
        if down:

            @pl.when(z > 0)
            def _():
                act(zz, c, 0, {"heads": z - 1}, **options)

        if up:

            @pl.when(z < count - 1)
            def _():
                act(zz, c, 1, {"heads": z + 1}, **options)

        act(zz, c, 2, {"ctx": across}, **options)
        act(zz, c, 3, {"ctx": beside}, **options)

    mine = c * count + z
    local = [
        pltpu.make_async_copy(x_ref, rows_ref.at[mine], own_sem.at[0]),
        pltpu.make_async_copy(t_ref, table_ref.at[mine], own_sem.at[1]),
    ]
    for copy in local:
        copy.start()
    along(start, True, True, z, own=True)

    def over(zz):
        arrived(zz, across)
        start(zz, across, 3, {"ctx": beside})

    for d in range(1, count + 1):
        if d < count:

            @pl.when(z >= d)
            def _():
                arrived(z - d, c)
                along(start, False, True, z - d)

            @pl.when(z + d < count)
            def _():
                arrived(z + d, c)
                along(start, True, False, z + d)

        if d == 1:
            over(z)
        else:

            @pl.when(z >= d - 1)
            def _():
                over(z - d + 1)

            @pl.when(z + d - 1 < count)
            def _():
                over(z + d - 1)

    for zz in range(count):
        arrived(zz, beside)
        arrived(zz, diagonal)
    for copy in local:
        copy.wait()
    along(left, True, True, z)
    for d in range(1, count):

        @pl.when(z >= d)
        def _():
            along(left, False, True, z - d)

        @pl.when(z + d < count)
        def _():
            along(left, True, False, z + d)

    for zz in range(count):
        left(zz, across, 3, {"ctx": beside})


def scatter_kernel(
    count, part_ref, out_ref, from_beside, from_across, below, above, to_across, to_line,
    beside_send, beside_recv, across_send, across_recv, line_send, below_recv, above_recv,
):
    z, c, beside, across, diagonal = place(count)
    greet(z, count, beside, across)

    def by_distance(act):
        for d in range(count - 1, 0, -1):

            @pl.when(z + d < count)
            def _():
                act(z + d, 1)

            @pl.when(z >= d)
            def _():
                act(z - d, -1)

        act(z, 0)

    def beside_copy(kind, zz):
        cc = diagonal if kind == 0 else beside
        return pltpu.make_async_remote_copy(
            src_ref=part_ref.at[cc * count + zz],
            dst_ref=from_beside.at[kind, zz],
            send_sem=beside_send.at[kind, zz],
            recv_sem=beside_recv.at[kind, zz],
            device_id={"ctx": beside},
            device_id_type=MESH,
        )

    def across_copy(zz):
        return pltpu.make_async_remote_copy(
            src_ref=to_across.at[zz],
            dst_ref=from_across.at[zz],
            send_sem=across_send.at[zz],
            recv_sem=across_recv.at[zz],
            device_id={"ctx": across},
            device_id_type=MESH,
        )

    def up_copy(zz):
        return pltpu.make_async_remote_copy(
            src_ref=to_line.at[zz],
            dst_ref=below.at[zz],
            send_sem=line_send.at[zz],
            recv_sem=below_recv.at[zz],
            device_id={"heads": z + 1},
            device_id_type=MESH,
        )

    def down_copy(zz):
        return pltpu.make_async_remote_copy(
            src_ref=to_line.at[zz],
            dst_ref=above.at[zz],
            send_sem=line_send.at[zz],
            recv_sem=above_recv.at[zz],
            device_id={"heads": z - 1},
            device_id_type=MESH,
        )

    def add(target, sources):
        def chunk(index, _):
            rows = pl.ds(pl.multiple_of(index * ADD_ROWS, ADD_ROWS), ADD_ROWS)
            total = sources[0][rows, :].astype(jnp.float32)
            for source in sources[1:]:
                total = total + source[rows, :].astype(jnp.float32)
            target[rows, :] = total.astype(target.dtype)
            return 0

        lax.fori_loop(0, target.shape[0] // ADD_ROWS, chunk, 0)

    by_distance(lambda zz, side: beside_copy(0, zz).start())
    by_distance(lambda zz, side: beside_copy(1, zz).start())

    def pass_across(zz, side):
        beside_copy(0, zz).wait_recv()
        add(to_across.at[zz], [part_ref.at[across * count + zz], from_beside.at[0, zz]])
        across_copy(zz).start()

    by_distance(pass_across)

    def pass_line(zz, side):
        beside_copy(1, zz).wait_recv()
        across_copy(zz).wait_recv()
        sources = [part_ref.at[c * count + zz], from_beside.at[1, zz], from_across.at[zz]]
        if side == 0:
            add(out_ref, sources)

            @pl.when(z > 0)
            def _():
                up_copy(zz).wait_recv()
                add(out_ref, [out_ref, below.at[zz]])

            @pl.when(z < count - 1)
            def _():
                down_copy(zz).wait_recv()
                add(out_ref, [out_ref, above.at[zz]])

            return
        first = z == 0 if side > 0 else z == count - 1
        copy = up_copy if side > 0 else down_copy
        arriving = below if side > 0 else above

        @pl.when(first)
        def _():
            add(to_line.at[zz], sources)

        @pl.when(jnp.logical_not(first))
        def _():
            copy(zz).wait_recv()
            add(to_line.at[zz], sources + [arriving.at[zz]])

        copy(zz).start()

    by_distance(pass_line)

    def sent(zz, side):
        beside_copy(0, zz).wait_send()
        beside_copy(1, zz).wait_send()
        across_copy(zz).wait_send()
        if side > 0:
            up_copy(zz).wait_send()
        if side < 0:
            down_copy(zz).wait_send()

    by_distance(sent)


def gather_rows(normed, table):
    count, devices = lax.axis_size("heads"), lax.axis_size("heads") * lax.axis_size("ctx")
    return pl.pallas_call(
        functools.partial(gather_kernel, count),
        out_shape=[
            jax.ShapeDtypeStruct((devices,) + value.shape, value.dtype)
            for value in (normed, table)
        ],
        in_specs=[pl.BlockSpec(memory_space=pltpu.VMEM)] * 2,
        out_specs=[pl.BlockSpec(memory_space=pl.ANY)] * 2,
        scratch_shapes=[
            pltpu.SemaphoreType.DMA((4, devices)),
            pltpu.SemaphoreType.DMA((4, devices)),
            pltpu.SemaphoreType.DMA((devices,)),
            pltpu.SemaphoreType.DMA((devices,)),
            pltpu.SemaphoreType.DMA((2,)),
        ],
        compiler_params=pltpu.CompilerParams(collective_id=0, has_side_effects=True),
        name="gather_rows",
    )(normed, table)


def scatter_sums(parts):
    count = lax.axis_size("heads")
    _, rows, width = parts.shape
    block = (rows, width)
    dma = pltpu.SemaphoreType.DMA
    return pl.pallas_call(
        functools.partial(scatter_kernel, count),
        out_shape=jax.ShapeDtypeStruct(block, jnp.float32),
        in_specs=[pl.BlockSpec(memory_space=pltpu.VMEM)],
        out_specs=pl.BlockSpec(memory_space=pltpu.VMEM),
        scratch_shapes=[pltpu.VMEM((2, count) + block, parts.dtype)]
        + [pltpu.VMEM((count,) + block, parts.dtype)] * 5
        + [dma((2, count))] * 2
        + [dma((count,))] * 5,
        compiler_params=pltpu.CompilerParams(
            collective_id=1, has_side_effects=True, vmem_limit_bytes=VMEM_BYTES
        ),
        name="scatter_sums",
    )(parts)


def dense_experts(
    hidden_float, normed, w_gate, w_up, w_down, expert_ids, gate_weights, expert_count
):
    axes = ("ctx", "heads")
    exp_local = w_gate.shape[0]
    chosen = expert_ids[:, :, None] == jnp.arange(expert_count, dtype=jnp.int32)
    table = jnp.sum(jnp.where(chosen, gate_weights[:, :, None], 0.0), axis=1)
    first = lax.axis_index(axes) * exp_local
    rows, tables = gather_rows(normed, table.T)
    device_count, row_count, width = rows.shape
    rows = rows.reshape(device_count * row_count, width)
    total = None
    for e in range(exp_local):
        gate_act = jnp.dot(rows, w_gate[e], preferred_element_type=jnp.float32)
        up_act = jnp.dot(rows, w_up[e], preferred_element_type=jnp.float32)
        hid = (jax.nn.silu(gate_act) * up_act).astype(jnp.bfloat16)
        out_rows = jnp.dot(hid, w_down[e], preferred_element_type=jnp.float32)
        weight = lax.dynamic_slice_in_dim(tables, first + e, 1, 1).reshape(-1, 1)
        part = weight * out_rows
        total = part if total is None else total + part
    parts = total.astype(jnp.bfloat16).reshape(device_count, row_count, width)
    routed = scatter_sums(parts)
    return (hidden_float + routed).astype(jnp.bfloat16)


def on_device(
    tokens, state_in, past_kv, w_qkv, w_out, w_gate, w_up, w_down, expert_ids, gate_weights
):
    row_count, model_width = tokens.shape
    inner_width = w_qkv.shape[2]
    local_heads = inner_width // HDIM
    w_flat = w_qkv.reshape(model_width, 3 * inner_width)
    projected = jnp.dot(
        lax.all_gather(tokens, "heads", axis=0, tiled=True),
        w_flat,
        preferred_element_type=jnp.float32,
    ).astype(jnp.bfloat16)
    slab_rows = projected.shape[0]
    projected = projected.reshape(slab_rows, 3, local_heads, HDIM)
    query = jnp.transpose(projected[:, 0], (1, 0, 2))
    keys = jnp.transpose(projected[:, 1], (1, 0, 2))
    values = jnp.transpose(projected[:, 2], (1, 0, 2))
    local_state = jnp.einsum("hsd,hse->hde", keys, values, preferred_element_type=jnp.float32)
    earlier_state = entering(
        local_state, "ctx", lambda first, second: first + second, jnp.zeros_like(local_state)
    )
    start_state = state_in + earlier_state
    tail = jnp.stack([keys, values], axis=0)
    arrived = from_behind(tail, "ctx", 1)
    past = jnp.transpose(past_kv.reshape(2, WINDOW, local_heads, HDIM), (0, 2, 1, 3))
    previous = jnp.where(lax.axis_index("ctx") == 0, past, arrived)
    all_keys = jnp.concatenate([previous[0], keys], axis=1)
    all_values = jnp.concatenate([previous[1], values], axis=1)
    block_rows = min(slab_rows, 512)
    block_count = slab_rows // block_rows
    scale = 1.0 / math.sqrt(HDIM)
    causal = jnp.arange(block_rows)[:, None] >= jnp.arange(block_rows)[None, :]
    offsets = jnp.arange(WINDOW + block_rows)[None, :] - jnp.arange(block_rows)[:, None]
    in_window = (offsets > 0) & (offsets <= WINDOW)

    def block_step(state, index):
        first = index * block_rows
        carried = jnp.einsum(
            "hsd,hde->hse", query.astype(jnp.float32), state, precision=lax.Precision.HIGHEST
        )
        inside = jnp.einsum("hsd,htd->hst", query, keys, preferred_element_type=jnp.float32)
        inside = jnp.where(causal[None], inside, 0.0).astype(jnp.bfloat16)
        linear = carried + jnp.einsum(
            "hst,hte->hse", inside, values, preferred_element_type=jnp.float32
        )
        scores = (
            jnp.einsum("hsd,htd->hst", query, all_keys, preferred_element_type=jnp.float32) * scale
        )
        scores = jnp.where(in_window[None], scores, -jnp.inf)
        top_score = jnp.max(scores, axis=-1, keepdims=True)
        expo = jnp.exp(scores - top_score)
        probs = (expo / jnp.sum(expo, axis=-1, keepdims=True)).astype(jnp.bfloat16)
        window_out = jnp.einsum(
            "hst,hte->hse", probs, all_values, preferred_element_type=jnp.float32
        )
        combined = (normalize(linear) + window_out).astype(jnp.bfloat16)
        new_state = state + jnp.einsum(
            "hsd,hse->hde", keys, values, preferred_element_type=jnp.float32
        )
        return (new_state, combined)

    _, outs = lax.scan(block_step, start_state, jnp.arange(block_count, dtype=jnp.int32))
    heads_out = jnp.transpose(outs, (0, 2, 1, 3)).reshape(slab_rows, inner_width)
    regrouped = lax.all_to_all(heads_out, "heads", split_axis=0, concat_axis=1, tiled=True)
    attn = jnp.dot(
        regrouped,
        lax.all_gather(w_out, "heads", axis=0, tiled=True),
        preferred_element_type=jnp.float32,
    )
    hidden_state = (tokens.astype(jnp.float32) + attn).astype(jnp.bfloat16)
    hidden_float = hidden_state.astype(jnp.float32)
    normed = normalize(hidden_float).astype(jnp.bfloat16)
    ctx_count = lax.axis_size("ctx")
    head_count = lax.axis_size("heads")
    exp_local = w_gate.shape[0]
    expert_count = exp_local * ctx_count * head_count
    top_count = expert_ids.shape[1]
    capacity = max(2, 2 * row_count * top_count // expert_count)
    devices = ctx_count * head_count
    if ctx_count == 4 and row_count * devices <= expert_count * capacity:
        return dense_experts(
            hidden_float, normed, w_gate, w_up, w_down, expert_ids, gate_weights, expert_count
        )
    picks = expert_ids.reshape(-1)
    onehot = (picks[:, None] == jnp.arange(expert_count, dtype=jnp.int32)[None, :]).astype(
        jnp.int32
    )
    earlier = jnp.cumsum(onehot, axis=0) - onehot
    slots = jnp.sum(onehot * earlier, axis=1)
    destination = picks * capacity + slots
    source_rows = jnp.arange(row_count * top_count, dtype=jnp.int32) // top_count
    outgoing = jnp.zeros((expert_count * capacity, model_width), jnp.bfloat16)
    outgoing = outgoing.at[destination].set(normed[source_rows])
    sendable = outgoing.reshape(expert_count, 1, capacity, model_width)
    arrived_rows = lax.all_to_all(
        sendable, ("ctx", "heads"), split_axis=0, concat_axis=1, tiled=True
    )
    e_count, n_count, c_count, d_count = arrived_rows.shape
    flat = arrived_rows.reshape(e_count, n_count * c_count, d_count)
    gate_act = jnp.einsum("erd,edf->erf", flat, w_gate, preferred_element_type=jnp.float32)
    up_act = jnp.einsum("erd,edf->erf", flat, w_up, preferred_element_type=jnp.float32)
    hid = (jax.nn.silu(gate_act) * up_act).astype(jnp.bfloat16)
    out_rows = jnp.einsum("erf,efd->erd", hid, w_down, preferred_element_type=jnp.float32)
    finished = out_rows.astype(jnp.bfloat16).reshape(e_count, n_count, c_count, d_count)
    returned = lax.all_to_all(finished, ("ctx", "heads"), split_axis=1, concat_axis=0, tiled=True)
    returned = returned.reshape(expert_count * capacity, model_width)
    picked = returned[destination].reshape(row_count, top_count, model_width).astype(jnp.float32)
    routed = jnp.sum(gate_weights[:, :, None] * picked, axis=1)
    return (hidden_float + routed).astype(jnp.bfloat16)


def solution(mesh):
    return jax.shard_map(
        on_device,
        mesh=mesh,
        in_specs=(
            P(("groups", "ctx", "heads"), None),
            P("heads", "groups", None),
            P(None, "groups", "heads"),
            P(None, None, "heads"),
            P("heads", None),
            P(("ctx", "heads"), None, None),
            P(("ctx", "heads"), None, None),
            P(("ctx", "heads"), None, None),
            P(("groups", "ctx", "heads"), None),
            P(("groups", "ctx", "heads"), None),
        ),
        out_specs=P(("groups", "ctx", "heads"), None),
        check_vma=False,
    )
```

```python
import functools
import math

import jax
import jax.numpy as jnp
from jax import lax
from jax.experimental import pallas as pl
from jax.experimental.pallas import tpu as pltpu
from jax.sharding import PartitionSpec as P

HDIM = 128
WINDOW = 512


def entering(x, axis, join, neutral):
    place = lax.axis_index(axis)
    gathered = lax.all_gather(x.astype(jnp.bfloat16), axis)
    state = jnp.zeros_like(x) + jnp.asarray(neutral, x.dtype)

    def one(lap, state):
        return join(state, lax.dynamic_index_in_dim(gathered, lap, 0, False).astype(x.dtype))

    return lax.fori_loop(0, place, one, state)


def from_behind(block, axis, distance):
    devices = range(lax.axis_size(axis))
    route = [(i - distance, i) for i in devices if i - distance in devices]
    return lax.ppermute(block, axis, route)


def normalize(value):
    return value * lax.rsqrt(jnp.mean(value * value, axis=-1, keepdims=True) + 1e-06)


MESH = pl.DeviceIdType.MESH
VMEM_BYTES = 60 * 1024 * 1024
ADD_ROWS = 16
DOT_COLUMNS = 512


def place(count):
    z = lax.axis_index("heads")
    c = lax.axis_index("ctx")
    beside = c + 1 - 2 * lax.rem(c, 2)
    across = lax.rem(c + 2, 4)
    diagonal = lax.rem(beside + 2, 4)
    return z, c, beside, across, diagonal


def greet(z, count, beside, across):
    barrier = pltpu.get_barrier_semaphore()

    def signal(target):
        pl.semaphore_signal(barrier, inc=1, device_id=target, device_id_type=MESH)

    signal({"ctx": beside})
    signal({"ctx": across})

    @pl.when(z > 0)
    def _():
        signal({"heads": z - 1})

    @pl.when(z < count - 1)
    def _():
        signal({"heads": z + 1})

    pl.semaphore_wait(barrier, 2 + jnp.minimum(z, 1) + jnp.minimum(count - 1 - z, 1))


def gather_kernel(
    count, x_ref, t_ref, rows_ref, table_ref, send_x, send_t, recv_x, recv_t, own_sem
):
    z, c, beside, across, diagonal = place(count)
    greet(z, count, beside, across)

    def copies(zz, cc, way, target, own=False):
        slot = cc * count + zz
        return [
            pltpu.make_async_remote_copy(
                src_ref=source if own else full.at[slot],
                dst_ref=full.at[slot],
                send_sem=send.at[way, slot],
                recv_sem=recv.at[slot],
                device_id=target,
                device_id_type=MESH,
            )
            for source, full, send, recv in (
                (x_ref, rows_ref, send_x, recv_x),
                (t_ref, table_ref, send_t, recv_t),
            )
        ]

    def start(zz, cc, way, target, own=False):
        for copy in copies(zz, cc, way, target, own):
            copy.start()

    def arrived(zz, cc):
        for copy in copies(zz, cc, 0, {"ctx": beside}):
            copy.wait_recv()

    def left(zz, cc, way, target):
        for copy in copies(zz, cc, way, target):
            copy.wait_send()

    def along(act, down, up, zz, **options):
        if down:

            @pl.when(z > 0)
            def _():
                act(zz, c, 0, {"heads": z - 1}, **options)

        if up:

            @pl.when(z < count - 1)
            def _():
                act(zz, c, 1, {"heads": z + 1}, **options)

        act(zz, c, 2, {"ctx": across}, **options)
        act(zz, c, 3, {"ctx": beside}, **options)

    mine = c * count + z
    local = [
        pltpu.make_async_copy(x_ref, rows_ref.at[mine], own_sem.at[0]),
        pltpu.make_async_copy(t_ref, table_ref.at[mine], own_sem.at[1]),
    ]
    for copy in local:
        copy.start()
    along(start, True, True, z, own=True)

    def over(zz):
        arrived(zz, across)
        start(zz, across, 3, {"ctx": beside})

    for d in range(1, count + 1):
        if d < count:

            @pl.when(z >= d)
            def _():
                arrived(z - d, c)
                along(start, False, True, z - d)

            @pl.when(z + d < count)
            def _():
                arrived(z + d, c)
                along(start, True, False, z + d)

        if d == 1:
            over(z)
        else:

            @pl.when(z >= d - 1)
            def _():
                over(z - d + 1)

            @pl.when(z + d - 1 < count)
            def _():
                over(z + d - 1)

    for zz in range(count):
        arrived(zz, beside)
        arrived(zz, diagonal)
    for copy in local:
        copy.wait()
    along(left, True, True, z)
    for d in range(1, count):

        @pl.when(z >= d)
        def _():
            along(left, False, True, z - d)

        @pl.when(z + d < count)
        def _():
            along(left, True, False, z + d)

    for zz in range(count):
        left(zz, across, 3, {"ctx": beside})


def scatter_kernel(
    count, hid_ref, down_ref, out_ref, part_ref, from_beside, from_across, below, above, to_across, to_line,
    beside_send, beside_recv, across_send, across_recv, line_send, below_recv, above_recv,
):
    z, c, beside, across, diagonal = place(count)
    greet(z, count, beside, across)

    def by_distance(act):
        for d in range(count - 1, 0, -1):

            @pl.when(z + d < count)
            def _():
                act(z + d, 1)

        for d in range(count - 1, 0, -1):

            @pl.when(z >= d)
            def _():
                act(z - d, -1)

        act(z, 0)

    def nth(index):
        ups = count - 1 - z
        downs = jnp.where(index < count - 1, index - ups, z)
        return jnp.where(index < ups, count - 1 - index, downs)

    def compute(slot):
        def tile(index, _):
            columns = pl.ds(pl.multiple_of(index * DOT_COLUMNS, DOT_COLUMNS), DOT_COLUMNS)
            part_ref[slot, :, columns] = jnp.dot(
                hid_ref[slot], down_ref[:, columns], preferred_element_type=jnp.float32
            ).astype(part_ref.dtype)
            return 0

        lax.fori_loop(0, down_ref.shape[1] // DOT_COLUMNS, tile, 0)

    def beside_copy(kind, zz):
        cc = diagonal if kind == 0 else beside
        return pltpu.make_async_remote_copy(
            src_ref=part_ref.at[cc * count + zz],
            dst_ref=from_beside.at[kind, zz],
            send_sem=beside_send.at[kind, zz],
            recv_sem=beside_recv.at[kind, zz],
            device_id={"ctx": beside},
            device_id_type=MESH,
        )

    def across_copy(zz):
        return pltpu.make_async_remote_copy(
            src_ref=to_across.at[zz],
            dst_ref=from_across.at[zz],
            send_sem=across_send.at[zz],
            recv_sem=across_recv.at[zz],
            device_id={"ctx": across},
            device_id_type=MESH,
        )

    def up_copy(zz):
        return pltpu.make_async_remote_copy(
            src_ref=to_line.at[zz],
            dst_ref=below.at[zz],
            send_sem=line_send.at[zz],
            recv_sem=below_recv.at[zz],
            device_id={"heads": z + 1},
            device_id_type=MESH,
        )

    def down_copy(zz):
        return pltpu.make_async_remote_copy(
            src_ref=to_line.at[zz],
            dst_ref=above.at[zz],
            send_sem=line_send.at[zz],
            recv_sem=above_recv.at[zz],
            device_id={"heads": z - 1},
            device_id_type=MESH,
        )

    def add(target, sources):
        def chunk(index, _):
            rows = pl.ds(pl.multiple_of(index * ADD_ROWS, ADD_ROWS), ADD_ROWS)
            total = sources[0][rows, :].astype(jnp.float32)
            for source in sources[1:]:
                total = total + source[rows, :].astype(jnp.float32)
            target[rows, :] = total.astype(target.dtype)
            return 0

        lax.fori_loop(0, target.shape[0] // ADD_ROWS, chunk, 0)

    def project(index, _):
        zz = nth(index)
        compute(diagonal * count + zz)
        beside_copy(0, zz).start()
        compute(across * count + zz)
        beside_copy(0, zz).wait_recv()
        add(to_across.at[zz], [part_ref.at[across * count + zz], from_beside.at[0, zz]])
        across_copy(zz).start()
        compute(beside * count + zz)
        beside_copy(1, zz).start()
        compute(c * count + zz)
        return 0

    lax.fori_loop(0, count, project, 0)

    def pass_line(zz, side):
        beside_copy(1, zz).wait_recv()
        across_copy(zz).wait_recv()
        sources = [part_ref.at[c * count + zz], from_beside.at[1, zz], from_across.at[zz]]
        if side == 0:
            add(out_ref, sources)

            @pl.when(z > 0)
            def _():
                up_copy(zz).wait_recv()
                add(out_ref, [out_ref, below.at[zz]])

            @pl.when(z < count - 1)
            def _():
                down_copy(zz).wait_recv()
                add(out_ref, [out_ref, above.at[zz]])

            return
        first = z == 0 if side > 0 else z == count - 1
        copy = up_copy if side > 0 else down_copy
        arriving = below if side > 0 else above

        @pl.when(first)
        def _():
            add(to_line.at[zz], sources)

        @pl.when(jnp.logical_not(first))
        def _():
            copy(zz).wait_recv()
            add(to_line.at[zz], sources + [arriving.at[zz]])

        copy(zz).start()

    by_distance(pass_line)

    def sent(zz, side):
        beside_copy(0, zz).wait_send()
        beside_copy(1, zz).wait_send()
        across_copy(zz).wait_send()
        if side > 0:
            up_copy(zz).wait_send()
        if side < 0:
            down_copy(zz).wait_send()

    by_distance(sent)


def gather_rows(normed, table):
    count, devices = lax.axis_size("heads"), lax.axis_size("heads") * lax.axis_size("ctx")
    return pl.pallas_call(
        functools.partial(gather_kernel, count),
        out_shape=[
            jax.ShapeDtypeStruct((devices,) + value.shape, value.dtype)
            for value in (normed, table)
        ],
        in_specs=[pl.BlockSpec(memory_space=pltpu.VMEM)] * 2,
        out_specs=[pl.BlockSpec(memory_space=pl.ANY)] * 2,
        scratch_shapes=[
            pltpu.SemaphoreType.DMA((4, devices)),
            pltpu.SemaphoreType.DMA((4, devices)),
            pltpu.SemaphoreType.DMA((devices,)),
            pltpu.SemaphoreType.DMA((devices,)),
            pltpu.SemaphoreType.DMA((2,)),
        ],
        compiler_params=pltpu.CompilerParams(collective_id=0, has_side_effects=True),
        name="gather_rows",
    )(normed, table)


def scatter_sums(hid, down):
    count = lax.axis_size("heads")
    devices, rows, _ = hid.shape
    block = (rows, down.shape[1])
    dma = pltpu.SemaphoreType.DMA
    return pl.pallas_call(
        functools.partial(scatter_kernel, count),
        out_shape=jax.ShapeDtypeStruct(block, jnp.float32),
        in_specs=[pl.BlockSpec(memory_space=pltpu.VMEM)] * 2,
        out_specs=pl.BlockSpec(memory_space=pltpu.VMEM),
        scratch_shapes=[
            pltpu.VMEM((devices,) + block, hid.dtype),
            pltpu.VMEM((2, count) + block, hid.dtype),
        ]
        + [pltpu.VMEM((count,) + block, hid.dtype)] * 5
        + [dma((2, count))] * 2
        + [dma((count,))] * 5,
        compiler_params=pltpu.CompilerParams(
            collective_id=1, has_side_effects=True, vmem_limit_bytes=VMEM_BYTES
        ),
        name="scatter_sums",
    )(hid, down)


def whole_rows(w_out):
    ctx_count, rows = lax.axis_size("ctx"), w_out.shape[0]
    share = rows // ctx_count
    if rows % ctx_count or share % 16:
        return lax.all_gather(w_out, "heads", axis=0, tiled=True)
    mine = lax.dynamic_slice_in_dim(w_out, lax.axis_index("ctx") * share, share, 0)
    return lax.all_gather(mine, ("heads", "ctx"), axis=0, tiled=True)


def dense_experts(
    hidden_float, normed, w_gate, w_up, w_down, expert_ids, gate_weights, expert_count
):
    axes = ("ctx", "heads")
    exp_local = w_gate.shape[0]
    chosen = expert_ids[:, :, None] == jnp.arange(expert_count, dtype=jnp.int32)
    table = jnp.sum(jnp.where(chosen, gate_weights[:, :, None], 0.0), axis=1)
    first = lax.axis_index(axes) * exp_local
    rows, tables = gather_rows(normed, table.T)
    device_count, row_count, width = rows.shape
    rows = rows.reshape(device_count * row_count, width)
    hids = []
    for e in range(exp_local):
        gate_act = jnp.dot(rows, w_gate[e], preferred_element_type=jnp.float32)
        up_act = jnp.dot(rows, w_up[e], preferred_element_type=jnp.float32)
        weight = lax.dynamic_slice_in_dim(tables, first + e, 1, 1).reshape(-1, 1)
        hids.append((weight * (jax.nn.silu(gate_act) * up_act)).astype(jnp.bfloat16))
    hid = jnp.concatenate(hids, axis=1) if exp_local > 1 else hids[0]
    routed = scatter_sums(
        hid.reshape(device_count, row_count, hid.shape[1]), w_down.reshape(hid.shape[1], width)
    )
    return (hidden_float + routed).astype(jnp.bfloat16)


def on_device(
    tokens, state_in, past_kv, w_qkv, w_out, w_gate, w_up, w_down, expert_ids, gate_weights
):
    row_count, model_width = tokens.shape
    inner_width = w_qkv.shape[2]
    local_heads = inner_width // HDIM
    w_flat = w_qkv.reshape(model_width, 3 * inner_width)
    projected = jnp.dot(
        lax.all_gather(tokens, "heads", axis=0, tiled=True),
        w_flat,
        preferred_element_type=jnp.float32,
    ).astype(jnp.bfloat16)
    slab_rows = projected.shape[0]
    projected = projected.reshape(slab_rows, 3, local_heads, HDIM)
    query = jnp.transpose(projected[:, 0], (1, 0, 2))
    keys = jnp.transpose(projected[:, 1], (1, 0, 2))
    values = jnp.transpose(projected[:, 2], (1, 0, 2))
    local_state = jnp.einsum("hsd,hse->hde", keys, values, preferred_element_type=jnp.float32)
    earlier_state = entering(
        local_state, "ctx", lambda first, second: first + second, jnp.zeros_like(local_state)
    )
    start_state = state_in + earlier_state
    tail = jnp.stack([keys, values], axis=0)
    arrived = from_behind(tail, "ctx", 1)
    past = jnp.transpose(past_kv.reshape(2, WINDOW, local_heads, HDIM), (0, 2, 1, 3))
    previous = jnp.where(lax.axis_index("ctx") == 0, past, arrived)
    all_keys = jnp.concatenate([previous[0], keys], axis=1)
    all_values = jnp.concatenate([previous[1], values], axis=1)
    block_rows = min(slab_rows, 512)
    block_count = slab_rows // block_rows
    scale = 1.0 / math.sqrt(HDIM)
    causal = jnp.arange(block_rows)[:, None] >= jnp.arange(block_rows)[None, :]
    offsets = jnp.arange(WINDOW + block_rows)[None, :] - jnp.arange(block_rows)[:, None]
    in_window = (offsets > 0) & (offsets <= WINDOW)

    def block_step(state, index):
        first = index * block_rows
        carried = jnp.einsum(
            "hsd,hde->hse", query.astype(jnp.float32), state, precision=lax.Precision.HIGHEST
        )
        inside = jnp.einsum("hsd,htd->hst", query, keys, preferred_element_type=jnp.float32)
        inside = jnp.where(causal[None], inside, 0.0).astype(jnp.bfloat16)
        linear = carried + jnp.einsum(
            "hst,hte->hse", inside, values, preferred_element_type=jnp.float32
        )
        scores = (
            jnp.einsum("hsd,htd->hst", query, all_keys, preferred_element_type=jnp.float32) * scale
        )
        scores = jnp.where(in_window[None], scores, -jnp.inf)
        top_score = jnp.max(scores, axis=-1, keepdims=True)
        expo = jnp.exp(scores - top_score)
        probs = (expo / jnp.sum(expo, axis=-1, keepdims=True)).astype(jnp.bfloat16)
        window_out = jnp.einsum(
            "hst,hte->hse", probs, all_values, preferred_element_type=jnp.float32
        )
        combined = (normalize(linear) + window_out).astype(jnp.bfloat16)
        new_state = state + jnp.einsum(
            "hsd,hse->hde", keys, values, preferred_element_type=jnp.float32
        )
        return (new_state, combined)

    _, outs = lax.scan(block_step, start_state, jnp.arange(block_count, dtype=jnp.int32))
    heads_out = jnp.transpose(outs, (0, 2, 1, 3)).reshape(slab_rows, inner_width)
    regrouped = lax.all_to_all(heads_out, "heads", split_axis=0, concat_axis=1, tiled=True)
    attn = jnp.dot(
        regrouped,
        whole_rows(w_out),
        preferred_element_type=jnp.float32,
    )
    hidden_state = (tokens.astype(jnp.float32) + attn).astype(jnp.bfloat16)
    hidden_float = hidden_state.astype(jnp.float32)
    normed = normalize(hidden_float).astype(jnp.bfloat16)
    ctx_count = lax.axis_size("ctx")
    head_count = lax.axis_size("heads")
    exp_local = w_gate.shape[0]
    expert_count = exp_local * ctx_count * head_count
    top_count = expert_ids.shape[1]
    capacity = max(2, 2 * row_count * top_count // expert_count)
    devices = ctx_count * head_count
    if ctx_count == 4 and row_count * devices <= expert_count * capacity:
        return dense_experts(
            hidden_float, normed, w_gate, w_up, w_down, expert_ids, gate_weights, expert_count
        )
    picks = expert_ids.reshape(-1)
    onehot = (picks[:, None] == jnp.arange(expert_count, dtype=jnp.int32)[None, :]).astype(
        jnp.int32
    )
    earlier = jnp.cumsum(onehot, axis=0) - onehot
    slots = jnp.sum(onehot * earlier, axis=1)
    destination = picks * capacity + slots
    source_rows = jnp.arange(row_count * top_count, dtype=jnp.int32) // top_count
    outgoing = jnp.zeros((expert_count * capacity, model_width), jnp.bfloat16)
    outgoing = outgoing.at[destination].set(normed[source_rows])
    sendable = outgoing.reshape(expert_count, 1, capacity, model_width)
    arrived_rows = lax.all_to_all(
        sendable, ("ctx", "heads"), split_axis=0, concat_axis=1, tiled=True
    )
    e_count, n_count, c_count, d_count = arrived_rows.shape
    flat = arrived_rows.reshape(e_count, n_count * c_count, d_count)
    gate_act = jnp.einsum("erd,edf->erf", flat, w_gate, preferred_element_type=jnp.float32)
    up_act = jnp.einsum("erd,edf->erf", flat, w_up, preferred_element_type=jnp.float32)
    hid = (jax.nn.silu(gate_act) * up_act).astype(jnp.bfloat16)
    out_rows = jnp.einsum("erf,efd->erd", hid, w_down, preferred_element_type=jnp.float32)
    finished = out_rows.astype(jnp.bfloat16).reshape(e_count, n_count, c_count, d_count)
    returned = lax.all_to_all(finished, ("ctx", "heads"), split_axis=1, concat_axis=0, tiled=True)
    returned = returned.reshape(expert_count * capacity, model_width)
    picked = returned[destination].reshape(row_count, top_count, model_width).astype(jnp.float32)
    routed = jnp.sum(gate_weights[:, :, None] * picked, axis=1)
    return (hidden_float + routed).astype(jnp.bfloat16)


def solution(mesh):
    return jax.shard_map(
        on_device,
        mesh=mesh,
        in_specs=(
            P(("groups", "ctx", "heads"), None),
            P("heads", "groups", None),
            P(None, "groups", "heads"),
            P(None, None, "heads"),
            P("heads", None),
            P(("ctx", "heads"), None, None),
            P(("ctx", "heads"), None, None),
            P(("ctx", "heads"), None, None),
            P(("groups", "ctx", "heads"), None),
            P(("groups", "ctx", "heads"), None),
        ),
        out_specs=P(("groups", "ctx", "heads"), None),
        check_vma=False,
    )
```

```python
import functools
import math

import jax
import jax.numpy as jnp
from jax import lax
from jax.experimental import pallas as pl
from jax.experimental.pallas import tpu as pltpu
from jax.sharding import PartitionSpec as P

HDIM = 128
WINDOW = 512


def entering(x, axis, join, neutral):
    place = lax.axis_index(axis)
    gathered = lax.all_gather(x.astype(jnp.bfloat16), axis)
    state = jnp.zeros_like(x) + jnp.asarray(neutral, x.dtype)

    def one(lap, state):
        return join(state, lax.dynamic_index_in_dim(gathered, lap, 0, False).astype(x.dtype))

    return lax.fori_loop(0, place, one, state)


def from_behind(block, axis, distance):
    devices = range(lax.axis_size(axis))
    route = [(i - distance, i) for i in devices if i - distance in devices]
    return lax.ppermute(block, axis, route)


def normalize(value):
    return value * lax.rsqrt(jnp.mean(value * value, axis=-1, keepdims=True) + 1e-06)


MESH = pl.DeviceIdType.MESH
VMEM_BYTES = 60 * 1024 * 1024
ADD_ROWS = 16
DOT_COLUMNS = 512
LAG = 2


def place(count):
    z = lax.axis_index("heads")
    c = lax.axis_index("ctx")
    beside = c + 1 - 2 * lax.rem(c, 2)
    across = lax.rem(c + 2, 4)
    diagonal = lax.rem(beside + 2, 4)
    return z, c, beside, across, diagonal


def greet(z, count, beside, across):
    barrier = pltpu.get_barrier_semaphore()

    def signal(target):
        pl.semaphore_signal(barrier, inc=1, device_id=target, device_id_type=MESH)

    signal({"ctx": beside})
    signal({"ctx": across})

    @pl.when(z > 0)
    def _():
        signal({"heads": z - 1})

    @pl.when(z < count - 1)
    def _():
        signal({"heads": z + 1})

    pl.semaphore_wait(barrier, 2 + jnp.minimum(z, 1) + jnp.minimum(count - 1 - z, 1))


def gather_kernel(
    count, x_ref, t_ref, rows_ref, table_ref, send_x, send_t, recv_x, recv_t, own_sem
):
    z, c, beside, across, diagonal = place(count)
    greet(z, count, beside, across)

    def copies(zz, cc, way, target, own=False):
        slot = cc * count + zz
        return [
            pltpu.make_async_remote_copy(
                src_ref=source if own else full.at[slot],
                dst_ref=full.at[slot],
                send_sem=send.at[way, slot],
                recv_sem=recv.at[slot],
                device_id=target,
                device_id_type=MESH,
            )
            for source, full, send, recv in (
                (x_ref, rows_ref, send_x, recv_x),
                (t_ref, table_ref, send_t, recv_t),
            )
        ]

    def start(zz, cc, way, target, own=False):
        for copy in copies(zz, cc, way, target, own):
            copy.start()

    def arrived(zz, cc):
        for copy in copies(zz, cc, 0, {"ctx": beside}):
            copy.wait_recv()

    def left(zz, cc, way, target):
        for copy in copies(zz, cc, way, target):
            copy.wait_send()

    def along(act, down, up, zz, **options):
        if down:

            @pl.when(z > 0)
            def _():
                act(zz, c, 0, {"heads": z - 1}, **options)

        if up:

            @pl.when(z < count - 1)
            def _():
                act(zz, c, 1, {"heads": z + 1}, **options)

        act(zz, c, 2, {"ctx": across}, **options)
        act(zz, c, 3, {"ctx": beside}, **options)

    mine = c * count + z
    local = [
        pltpu.make_async_copy(x_ref, rows_ref.at[mine], own_sem.at[0]),
        pltpu.make_async_copy(t_ref, table_ref.at[mine], own_sem.at[1]),
    ]
    for copy in local:
        copy.start()
    along(start, True, True, z, own=True)

    def over(zz):
        arrived(zz, across)
        start(zz, across, 3, {"ctx": beside})

    for d in range(1, count + 1):
        if d < count:

            @pl.when(z >= d)
            def _():
                arrived(z - d, c)
                along(start, False, True, z - d)

            @pl.when(z + d < count)
            def _():
                arrived(z + d, c)
                along(start, True, False, z + d)

        if d == 1:
            over(z)
        else:

            @pl.when(z >= d - 1)
            def _():
                over(z - d + 1)

            @pl.when(z + d - 1 < count)
            def _():
                over(z + d - 1)

    for zz in range(count):
        arrived(zz, beside)
        arrived(zz, diagonal)
    for copy in local:
        copy.wait()
    along(left, True, True, z)
    for d in range(1, count):

        @pl.when(z >= d)
        def _():
            along(left, False, True, z - d)

        @pl.when(z + d < count)
        def _():
            along(left, True, False, z + d)

    for zz in range(count):
        left(zz, across, 3, {"ctx": beside})


def scatter_kernel(
    count, hid_ref, down_ref, weight_ref, out_ref, part_ref, from_beside, from_across, below, above, to_across, to_line,
    beside_send, beside_recv, across_send, across_recv, line_send, below_recv, above_recv,
):
    z, c, beside, across, diagonal = place(count)
    greet(z, count, beside, across)

    def nth(index):
        more = jnp.maximum(z, count - 1 - z)
        fewer = count - 1 - more
        alone = more - fewer
        paired = jnp.maximum(index - alone, 0)
        up = jnp.where(z + more < count, more - index, index - more)
        both = (fewer - paired // 2) * (1 - 2 * (paired % 2))
        offset = jnp.where(index < alone, up, both)
        return z + jnp.where(index < count - 1, offset, 0)

    def compute(slot):
        weight = weight_ref[slot][:, :1]

        def tile(index, _):
            columns = pl.ds(pl.multiple_of(index * DOT_COLUMNS, DOT_COLUMNS), DOT_COLUMNS)
            product = jnp.dot(
                hid_ref[slot], down_ref[:, columns], preferred_element_type=jnp.float32
            )
            part_ref[slot, :, columns] = (weight * product).astype(part_ref.dtype)
            return 0

        lax.fori_loop(0, down_ref.shape[1] // DOT_COLUMNS, tile, 0)

    def beside_copy(kind, zz):
        cc = diagonal if kind == 0 else beside
        return pltpu.make_async_remote_copy(
            src_ref=part_ref.at[cc * count + zz],
            dst_ref=from_beside.at[kind, zz],
            send_sem=beside_send.at[kind, zz],
            recv_sem=beside_recv.at[kind, zz],
            device_id={"ctx": beside},
            device_id_type=MESH,
        )

    def across_copy(zz):
        return pltpu.make_async_remote_copy(
            src_ref=to_across.at[zz],
            dst_ref=from_across.at[zz],
            send_sem=across_send.at[zz],
            recv_sem=across_recv.at[zz],
            device_id={"ctx": across},
            device_id_type=MESH,
        )

    def up_copy(zz):
        return pltpu.make_async_remote_copy(
            src_ref=to_line.at[zz],
            dst_ref=below.at[zz],
            send_sem=line_send.at[zz],
            recv_sem=below_recv.at[zz],
            device_id={"heads": z + 1},
            device_id_type=MESH,
        )

    def down_copy(zz):
        return pltpu.make_async_remote_copy(
            src_ref=to_line.at[zz],
            dst_ref=above.at[zz],
            send_sem=line_send.at[zz],
            recv_sem=above_recv.at[zz],
            device_id={"heads": z - 1},
            device_id_type=MESH,
        )

    def add(target, sources):
        def chunk(index, _):
            rows = pl.ds(pl.multiple_of(index * ADD_ROWS, ADD_ROWS), ADD_ROWS)
            total = sources[0][rows, :].astype(jnp.float32)
            for source in sources[1:]:
                total = total + source[rows, :].astype(jnp.float32)
            target[rows, :] = total.astype(target.dtype)
            return 0

        lax.fori_loop(0, target.shape[0] // ADD_ROWS, chunk, 0)

    def project(zz):
        compute(diagonal * count + zz)
        beside_copy(0, zz).start()
        compute(across * count + zz)
        beside_copy(0, zz).wait_recv()
        add(to_across.at[zz], [part_ref.at[across * count + zz], from_beside.at[0, zz]])
        across_copy(zz).start()
        compute(beside * count + zz)
        beside_copy(1, zz).start()
        compute(c * count + zz)

    def onward(zz, copy, arriving, first, sources):
        @pl.when(first)
        def _():
            add(to_line.at[zz], sources)

        @pl.when(jnp.logical_not(first))
        def _():
            copy(zz).wait_recv()
            add(to_line.at[zz], sources + [arriving.at[zz]])

        copy(zz).start()

    def pass_line(zz):
        beside_copy(1, zz).wait_recv()
        across_copy(zz).wait_recv()
        sources = [part_ref.at[c * count + zz], from_beside.at[1, zz], from_across.at[zz]]

        @pl.when(zz > z)
        def _():
            onward(zz, up_copy, below, z == 0, sources)

        @pl.when(zz < z)
        def _():
            onward(zz, down_copy, above, z == count - 1, sources)

        @pl.when(zz == z)
        def _():
            add(out_ref, sources)

            @pl.when(z > 0)
            def _():
                up_copy(zz).wait_recv()
                add(out_ref, [out_ref, below.at[zz]])

            @pl.when(z < count - 1)
            def _():
                down_copy(zz).wait_recv()
                add(out_ref, [out_ref, above.at[zz]])

    def step(index, _):
        @pl.when(index < count)
        def _():
            project(nth(index))

        @pl.when(index >= LAG)
        def _():
            pass_line(nth(index - LAG))

        return 0

    lax.fori_loop(0, count + LAG, step, 0)

    for zz in range(count):
        beside_copy(0, zz).wait_send()
        beside_copy(1, zz).wait_send()
        across_copy(zz).wait_send()

        @pl.when(zz > z)
        def _():
            up_copy(zz).wait_send()

        @pl.when(zz < z)
        def _():
            down_copy(zz).wait_send()


def gather_rows(normed, table):
    count, devices = lax.axis_size("heads"), lax.axis_size("heads") * lax.axis_size("ctx")
    return pl.pallas_call(
        functools.partial(gather_kernel, count),
        out_shape=[
            jax.ShapeDtypeStruct((devices,) + value.shape, value.dtype)
            for value in (normed, table)
        ],
        in_specs=[pl.BlockSpec(memory_space=pltpu.VMEM)] * 2,
        out_specs=[pl.BlockSpec(memory_space=pl.ANY)] * 2,
        scratch_shapes=[
            pltpu.SemaphoreType.DMA((4, devices)),
            pltpu.SemaphoreType.DMA((4, devices)),
            pltpu.SemaphoreType.DMA((devices,)),
            pltpu.SemaphoreType.DMA((devices,)),
            pltpu.SemaphoreType.DMA((2,)),
        ],
        compiler_params=pltpu.CompilerParams(collective_id=0, has_side_effects=True),
        name="gather_rows",
    )(normed, table)


def scatter_sums(hid, down, weights):
    count = lax.axis_size("heads")
    devices, rows, _ = hid.shape
    block = (rows, down.shape[1])
    dma = pltpu.SemaphoreType.DMA
    return pl.pallas_call(
        functools.partial(scatter_kernel, count),
        out_shape=jax.ShapeDtypeStruct(block, jnp.float32),
        in_specs=[pl.BlockSpec(memory_space=pltpu.VMEM)] * 3,
        out_specs=pl.BlockSpec(memory_space=pltpu.VMEM),
        scratch_shapes=[
            pltpu.VMEM((devices,) + block, hid.dtype),
            pltpu.VMEM((2, count) + block, hid.dtype),
        ]
        + [pltpu.VMEM((count,) + block, hid.dtype)] * 5
        + [dma((2, count))] * 2
        + [dma((count,))] * 5,
        compiler_params=pltpu.CompilerParams(
            collective_id=1, has_side_effects=True, vmem_limit_bytes=VMEM_BYTES
        ),
        name="scatter_sums",
    )(hid, down, weights)


def whole_rows(w_out):
    ctx_count, rows = lax.axis_size("ctx"), w_out.shape[0]
    share = rows // ctx_count
    if rows % ctx_count or share % 16:
        return lax.all_gather(w_out, "heads", axis=0, tiled=True)
    mine = lax.dynamic_slice_in_dim(w_out, lax.axis_index("ctx") * share, share, 0)
    return lax.all_gather(mine, ("heads", "ctx"), axis=0, tiled=True)


def dense_experts(
    hidden_float, normed, w_gate, w_up, w_down, expert_ids, gate_weights, expert_count
):
    axes = ("ctx", "heads")
    exp_local = w_gate.shape[0]
    chosen = expert_ids[:, :, None] == jnp.arange(expert_count, dtype=jnp.int32)
    table = jnp.sum(jnp.where(chosen, gate_weights[:, :, None], 0.0), axis=1)
    first = lax.axis_index(axes) * exp_local
    rows, tables = gather_rows(normed, table.T)
    device_count, row_count, width = rows.shape
    rows = rows.reshape(device_count * row_count, width)
    routed = 0.0
    for e in range(exp_local):
        gate_act = jnp.dot(rows, w_gate[e], preferred_element_type=jnp.float32)
        up_act = jnp.dot(rows, w_up[e], preferred_element_type=jnp.float32)
        hid = (jax.nn.silu(gate_act) * up_act).astype(jnp.bfloat16)
        weight = lax.dynamic_index_in_dim(tables, first + e, 1, False)
        weight = jnp.broadcast_to(weight[:, :, None], (device_count, row_count, HDIM))
        hid = hid.reshape(device_count, row_count, hid.shape[1])
        routed = routed + scatter_sums(hid, w_down[e], weight)
    return (hidden_float + routed).astype(jnp.bfloat16)


def on_device(
    tokens, state_in, past_kv, w_qkv, w_out, w_gate, w_up, w_down, expert_ids, gate_weights
):
    row_count, model_width = tokens.shape
    inner_width = w_qkv.shape[2]
    local_heads = inner_width // HDIM
    w_flat = w_qkv.reshape(model_width, 3 * inner_width)
    projected = jnp.dot(
        lax.all_gather(tokens, "heads", axis=0, tiled=True),
        w_flat,
        preferred_element_type=jnp.float32,
    ).astype(jnp.bfloat16)
    slab_rows = projected.shape[0]
    projected = projected.reshape(slab_rows, 3, local_heads, HDIM)
    query = jnp.transpose(projected[:, 0], (1, 0, 2))
    keys = jnp.transpose(projected[:, 1], (1, 0, 2))
    values = jnp.transpose(projected[:, 2], (1, 0, 2))
    local_state = jnp.einsum("hsd,hse->hde", keys, values, preferred_element_type=jnp.float32)
    earlier_state = entering(
        local_state, "ctx", lambda first, second: first + second, jnp.zeros_like(local_state)
    )
    start_state = state_in + earlier_state
    tail = jnp.stack([keys, values], axis=0)
    arrived = from_behind(tail, "ctx", 1)
    past = jnp.transpose(past_kv.reshape(2, WINDOW, local_heads, HDIM), (0, 2, 1, 3))
    previous = jnp.where(lax.axis_index("ctx") == 0, past, arrived)
    all_keys = jnp.concatenate([previous[0], keys], axis=1)
    all_values = jnp.concatenate([previous[1], values], axis=1)
    block_rows = min(slab_rows, 512)
    block_count = slab_rows // block_rows
    scale = 1.0 / math.sqrt(HDIM)
    causal = jnp.arange(block_rows)[:, None] >= jnp.arange(block_rows)[None, :]
    offsets = jnp.arange(WINDOW + block_rows)[None, :] - jnp.arange(block_rows)[:, None]
    in_window = (offsets > 0) & (offsets <= WINDOW)

    def block_step(state, index):
        first = index * block_rows
        carried = jnp.einsum(
            "hsd,hde->hse", query.astype(jnp.float32), state, precision=lax.Precision.HIGHEST
        )
        inside = jnp.einsum("hsd,htd->hst", query, keys, preferred_element_type=jnp.float32)
        inside = jnp.where(causal[None], inside, 0.0).astype(jnp.bfloat16)
        linear = carried + jnp.einsum(
            "hst,hte->hse", inside, values, preferred_element_type=jnp.float32
        )
        scores = (
            jnp.einsum("hsd,htd->hst", query, all_keys, preferred_element_type=jnp.float32) * scale
        )
        scores = jnp.where(in_window[None], scores, -jnp.inf)
        top_score = jnp.max(scores, axis=-1, keepdims=True)
        expo = jnp.exp(scores - top_score)
        probs = (expo / jnp.sum(expo, axis=-1, keepdims=True)).astype(jnp.bfloat16)
        window_out = jnp.einsum(
            "hst,hte->hse", probs, all_values, preferred_element_type=jnp.float32
        )
        combined = (normalize(linear) + window_out).astype(jnp.bfloat16)
        new_state = state + jnp.einsum(
            "hsd,hse->hde", keys, values, preferred_element_type=jnp.float32
        )
        return (new_state, combined)

    _, outs = lax.scan(block_step, start_state, jnp.arange(block_count, dtype=jnp.int32))
    heads_out = jnp.transpose(outs, (0, 2, 1, 3)).reshape(slab_rows, inner_width)
    regrouped = lax.all_to_all(heads_out, "heads", split_axis=0, concat_axis=1, tiled=True)
    attn = jnp.dot(
        regrouped,
        whole_rows(w_out),
        preferred_element_type=jnp.float32,
    )
    hidden_state = (tokens.astype(jnp.float32) + attn).astype(jnp.bfloat16)
    hidden_float = hidden_state.astype(jnp.float32)
    normed = normalize(hidden_float).astype(jnp.bfloat16)
    ctx_count = lax.axis_size("ctx")
    head_count = lax.axis_size("heads")
    exp_local = w_gate.shape[0]
    expert_count = exp_local * ctx_count * head_count
    top_count = expert_ids.shape[1]
    capacity = max(2, 2 * row_count * top_count // expert_count)
    devices = ctx_count * head_count
    if ctx_count == 4 and row_count * devices <= expert_count * capacity:
        return dense_experts(
            hidden_float, normed, w_gate, w_up, w_down, expert_ids, gate_weights, expert_count
        )
    picks = expert_ids.reshape(-1)
    onehot = (picks[:, None] == jnp.arange(expert_count, dtype=jnp.int32)[None, :]).astype(
        jnp.int32
    )
    earlier = jnp.cumsum(onehot, axis=0) - onehot
    slots = jnp.sum(onehot * earlier, axis=1)
    destination = picks * capacity + slots
    source_rows = jnp.arange(row_count * top_count, dtype=jnp.int32) // top_count
    outgoing = jnp.zeros((expert_count * capacity, model_width), jnp.bfloat16)
    outgoing = outgoing.at[destination].set(normed[source_rows])
    sendable = outgoing.reshape(expert_count, 1, capacity, model_width)
    arrived_rows = lax.all_to_all(
        sendable, ("ctx", "heads"), split_axis=0, concat_axis=1, tiled=True
    )
    e_count, n_count, c_count, d_count = arrived_rows.shape
    flat = arrived_rows.reshape(e_count, n_count * c_count, d_count)
    gate_act = jnp.einsum("erd,edf->erf", flat, w_gate, preferred_element_type=jnp.float32)
    up_act = jnp.einsum("erd,edf->erf", flat, w_up, preferred_element_type=jnp.float32)
    hid = (jax.nn.silu(gate_act) * up_act).astype(jnp.bfloat16)
    out_rows = jnp.einsum("erf,efd->erd", hid, w_down, preferred_element_type=jnp.float32)
    finished = out_rows.astype(jnp.bfloat16).reshape(e_count, n_count, c_count, d_count)
    returned = lax.all_to_all(finished, ("ctx", "heads"), split_axis=1, concat_axis=0, tiled=True)
    returned = returned.reshape(expert_count * capacity, model_width)
    picked = returned[destination].reshape(row_count, top_count, model_width).astype(jnp.float32)
    routed = jnp.sum(gate_weights[:, :, None] * picked, axis=1)
    return (hidden_float + routed).astype(jnp.bfloat16)


def solution(mesh):
    return jax.shard_map(
        on_device,
        mesh=mesh,
        in_specs=(
            P(("groups", "ctx", "heads"), None),
            P("heads", "groups", None),
            P(None, "groups", "heads"),
            P(None, None, "heads"),
            P("heads", None),
            P(("ctx", "heads"), None, None),
            P(("ctx", "heads"), None, None),
            P(("ctx", "heads"), None, None),
            P(("groups", "ctx", "heads"), None),
            P(("groups", "ctx", "heads"), None),
        ),
        out_specs=P(("groups", "ctx", "heads"), None),
        check_vma=False,
    )
```

```python
import functools
import math

import jax
import jax.numpy as jnp
from jax import lax
from jax.experimental import pallas as pl
from jax.experimental.pallas import tpu as pltpu
from jax.sharding import PartitionSpec as P

HDIM = 128
WINDOW = 512


def entering(x, axis, join, neutral):
    place = lax.axis_index(axis)
    gathered = lax.all_gather(x.astype(jnp.bfloat16), axis)
    state = jnp.zeros_like(x) + jnp.asarray(neutral, x.dtype)

    def one(lap, state):
        return join(state, lax.dynamic_index_in_dim(gathered, lap, 0, False).astype(x.dtype))

    return lax.fori_loop(0, place, one, state)


def from_behind(block, axis, distance):
    devices = range(lax.axis_size(axis))
    route = [(i - distance, i) for i in devices if i - distance in devices]
    return lax.ppermute(block, axis, route)


def normalize(value):
    return value * lax.rsqrt(jnp.mean(value * value, axis=-1, keepdims=True) + 1e-06)


MESH = pl.DeviceIdType.MESH
VMEM_BYTES = 60 * 1024 * 1024
ADD_ROWS = 16
DOT_COLUMNS = 512
LAG = 2


def place(count):
    z = lax.axis_index("heads")
    c = lax.axis_index("ctx")
    beside = c + 1 - 2 * lax.rem(c, 2)
    across = lax.rem(c + 2, 4)
    diagonal = lax.rem(beside + 2, 4)
    return z, c, beside, across, diagonal


def greet(z, count, beside, across):
    barrier = pltpu.get_barrier_semaphore()

    def signal(target):
        pl.semaphore_signal(barrier, inc=1, device_id=target, device_id_type=MESH)

    signal({"ctx": beside})
    signal({"ctx": across})

    @pl.when(z > 0)
    def _():
        signal({"heads": z - 1})

    @pl.when(z < count - 1)
    def _():
        signal({"heads": z + 1})

    pl.semaphore_wait(barrier, 2 + jnp.minimum(z, 1) + jnp.minimum(count - 1 - z, 1))


def gather_kernel(count, kinds, *refs):
    size = len(kinds)
    groups = [refs[first * size : (first + 1) * size] for first in range(4)]
    own_sem = refs[4 * size]
    z, c, beside, across, diagonal = place(count)
    greet(z, count, beside, across)

    def origin(kind, source, full):
        if kind != "share":
            return source
        share = full.shape[1]
        return source.at[pl.ds(pl.multiple_of(c * share, share), share), :]

    def slot_of(kind, zz, cc):
        return {"group": cc * count + zz, "share": zz * 4 + cc, "line": zz}[kind]

    def copies(zz, cc, way, target, own=False):
        result = []
        for kind, source, full, send, recv in zip(kinds, *groups):
            if kind == "line" and (way > 1 or cc is not c):
                continue
            slot = slot_of(kind, zz, cc)
            result.append(
                pltpu.make_async_remote_copy(
                    src_ref=origin(kind, source, full) if own else full.at[slot],
                    dst_ref=full.at[slot],
                    send_sem=send.at[way, slot],
                    recv_sem=recv.at[slot],
                    device_id=target,
                    device_id_type=MESH,
                )
            )
        return result

    def start(zz, cc, way, target, own=False):
        for copy in copies(zz, cc, way, target, own):
            copy.start()

    def arrived(zz, cc):
        for copy in copies(zz, cc, 0, {"ctx": beside}):
            copy.wait_recv()

    def left(zz, cc, way, target):
        for copy in copies(zz, cc, way, target):
            copy.wait_send()

    def along(act, down, up, zz, **options):
        if down:

            @pl.when(z > 0)
            def _():
                act(zz, c, 0, {"heads": z - 1}, **options)

        if up:

            @pl.when(z < count - 1)
            def _():
                act(zz, c, 1, {"heads": z + 1}, **options)

        act(zz, c, 2, {"ctx": across}, **options)
        act(zz, c, 3, {"ctx": beside}, **options)

    local = [
        pltpu.make_async_copy(
            origin(kind, source, full), full.at[slot_of(kind, z, c)], own_sem.at[index]
        )
        for index, (kind, source, full) in enumerate(zip(kinds, *groups[:2]))
    ]
    for copy in local:
        copy.start()
    along(start, True, True, z, own=True)

    def over(zz):
        arrived(zz, across)
        start(zz, across, 3, {"ctx": beside})

    for d in range(1, count + 1):
        if d < count:

            @pl.when(z >= d)
            def _():
                arrived(z - d, c)
                along(start, False, True, z - d)

            @pl.when(z + d < count)
            def _():
                arrived(z + d, c)
                along(start, True, False, z + d)

        if d == 1:
            over(z)
        else:

            @pl.when(z >= d - 1)
            def _():
                over(z - d + 1)

            @pl.when(z + d - 1 < count)
            def _():
                over(z + d - 1)

    for zz in range(count):
        arrived(zz, beside)
        arrived(zz, diagonal)
    for copy in local:
        copy.wait()
    along(left, True, True, z)
    for d in range(1, count):

        @pl.when(z >= d)
        def _():
            along(left, False, True, z - d)

        @pl.when(z + d < count)
        def _():
            along(left, True, False, z + d)

    for zz in range(count):
        left(zz, across, 3, {"ctx": beside})


def scatter_kernel(
    count, hid_ref, down_ref, weight_ref, out_ref, part_ref, from_beside, from_across, below, above, to_across, to_line,
    beside_send, beside_recv, across_send, across_recv, line_send, below_recv, above_recv,
):
    z, c, beside, across, diagonal = place(count)
    greet(z, count, beside, across)

    def nth(index):
        more = jnp.maximum(z, count - 1 - z)
        fewer = count - 1 - more
        alone = more - fewer
        paired = jnp.maximum(index - alone, 0)
        up = jnp.where(z + more < count, more - index, index - more)
        both = (fewer - paired // 2) * (1 - 2 * (paired % 2))
        offset = jnp.where(index < alone, up, both)
        return z + jnp.where(index < count - 1, offset, 0)

    def compute(slot):
        weight = weight_ref[slot][:, :1]

        def tile(index, _):
            columns = pl.ds(pl.multiple_of(index * DOT_COLUMNS, DOT_COLUMNS), DOT_COLUMNS)
            product = jnp.dot(
                hid_ref[slot], down_ref[:, columns], preferred_element_type=jnp.float32
            )
            part_ref[slot, :, columns] = (weight * product).astype(part_ref.dtype)
            return 0

        lax.fori_loop(0, down_ref.shape[1] // DOT_COLUMNS, tile, 0)

    def beside_copy(kind, zz):
        cc = diagonal if kind == 0 else beside
        return pltpu.make_async_remote_copy(
            src_ref=part_ref.at[cc * count + zz],
            dst_ref=from_beside.at[kind, zz],
            send_sem=beside_send.at[kind, zz],
            recv_sem=beside_recv.at[kind, zz],
            device_id={"ctx": beside},
            device_id_type=MESH,
        )

    def across_copy(zz):
        return pltpu.make_async_remote_copy(
            src_ref=to_across.at[zz],
            dst_ref=from_across.at[zz],
            send_sem=across_send.at[zz],
            recv_sem=across_recv.at[zz],
            device_id={"ctx": across},
            device_id_type=MESH,
        )

    def up_copy(zz):
        return pltpu.make_async_remote_copy(
            src_ref=to_line.at[zz],
            dst_ref=below.at[zz],
            send_sem=line_send.at[zz],
            recv_sem=below_recv.at[zz],
            device_id={"heads": z + 1},
            device_id_type=MESH,
        )

    def down_copy(zz):
        return pltpu.make_async_remote_copy(
            src_ref=to_line.at[zz],
            dst_ref=above.at[zz],
            send_sem=line_send.at[zz],
            recv_sem=above_recv.at[zz],
            device_id={"heads": z - 1},
            device_id_type=MESH,
        )

    def add(target, sources):
        def chunk(index, _):
            rows = pl.ds(pl.multiple_of(index * ADD_ROWS, ADD_ROWS), ADD_ROWS)
            total = sources[0][rows, :].astype(jnp.float32)
            for source in sources[1:]:
                total = total + source[rows, :].astype(jnp.float32)
            target[rows, :] = total.astype(target.dtype)
            return 0

        lax.fori_loop(0, target.shape[0] // ADD_ROWS, chunk, 0)

    def project(zz):
        compute(diagonal * count + zz)
        beside_copy(0, zz).start()
        compute(across * count + zz)
        beside_copy(0, zz).wait_recv()
        add(to_across.at[zz], [part_ref.at[across * count + zz], from_beside.at[0, zz]])
        across_copy(zz).start()
        compute(beside * count + zz)
        beside_copy(1, zz).start()
        compute(c * count + zz)

    def onward(zz, copy, arriving, first, sources):
        @pl.when(first)
        def _():
            add(to_line.at[zz], sources)

        @pl.when(jnp.logical_not(first))
        def _():
            copy(zz).wait_recv()
            add(to_line.at[zz], sources + [arriving.at[zz]])

        copy(zz).start()

    def pass_line(zz):
        beside_copy(1, zz).wait_recv()
        across_copy(zz).wait_recv()
        sources = [part_ref.at[c * count + zz], from_beside.at[1, zz], from_across.at[zz]]

        @pl.when(zz > z)
        def _():
            onward(zz, up_copy, below, z == 0, sources)

        @pl.when(zz < z)
        def _():
            onward(zz, down_copy, above, z == count - 1, sources)

        @pl.when(zz == z)
        def _():
            add(out_ref, sources)

            @pl.when(z > 0)
            def _():
                up_copy(zz).wait_recv()
                add(out_ref, [out_ref, below.at[zz]])

            @pl.when(z < count - 1)
            def _():
                down_copy(zz).wait_recv()
                add(out_ref, [out_ref, above.at[zz]])

    def step(index, _):
        @pl.when(index < count)
        def _():
            project(nth(index))

        @pl.when(index >= LAG)
        def _():
            pass_line(nth(index - LAG))

        return 0

    lax.fori_loop(0, count + LAG, step, 0)

    for zz in range(count):
        beside_copy(0, zz).wait_send()
        beside_copy(1, zz).wait_send()
        across_copy(zz).wait_send()

        @pl.when(zz > z)
        def _():
            up_copy(zz).wait_send()

        @pl.when(zz < z)
        def _():
            down_copy(zz).wait_send()


def gather_blocks(kinds, operands, collective_id, name):
    count, ctx_count = lax.axis_size("heads"), lax.axis_size("ctx")
    slots = [count if kind == "line" else count * ctx_count for kind in kinds]
    shapes = [
        (value.shape[0] // ctx_count if kind == "share" else value.shape[0], value.shape[1])
        for kind, value in zip(kinds, operands)
    ]
    return pl.pallas_call(
        functools.partial(gather_kernel, count, kinds),
        out_shape=[
            jax.ShapeDtypeStruct((slot,) + shape, value.dtype)
            for slot, shape, value in zip(slots, shapes, operands)
        ],
        in_specs=[pl.BlockSpec(memory_space=pltpu.VMEM)] * len(kinds),
        out_specs=[pl.BlockSpec(memory_space=pl.ANY)] * len(kinds),
        scratch_shapes=[pltpu.SemaphoreType.DMA((4, slot)) for slot in slots]
        + [pltpu.SemaphoreType.DMA((slot,)) for slot in slots]
        + [pltpu.SemaphoreType.DMA((len(kinds),))],
        compiler_params=pltpu.CompilerParams(
            collective_id=collective_id, has_side_effects=True
        ),
        name=name,
    )(*operands)


def scatter_sums(hid, down, weights):
    count = lax.axis_size("heads")
    devices, rows, _ = hid.shape
    block = (rows, down.shape[1])
    dma = pltpu.SemaphoreType.DMA
    return pl.pallas_call(
        functools.partial(scatter_kernel, count),
        out_shape=jax.ShapeDtypeStruct(block, jnp.float32),
        in_specs=[pl.BlockSpec(memory_space=pltpu.VMEM)] * 3,
        out_specs=pl.BlockSpec(memory_space=pltpu.VMEM),
        scratch_shapes=[
            pltpu.VMEM((devices,) + block, hid.dtype),
            pltpu.VMEM((2, count) + block, hid.dtype),
        ]
        + [pltpu.VMEM((count,) + block, hid.dtype)] * 5
        + [dma((2, count))] * 2
        + [dma((count,))] * 5,
        compiler_params=pltpu.CompilerParams(
            collective_id=1, has_side_effects=True, vmem_limit_bytes=VMEM_BYTES
        ),
        name="scatter_sums",
    )(hid, down, weights)


def gather_inputs(tokens, w_out):
    if lax.axis_size("ctx") == 4 and w_out.shape[0] % 64 == 0:
        slab, w_rows = gather_blocks(("line", "share"), (tokens, w_out), 2, "gather_inputs")
        width = tokens.shape[1]
        return slab.reshape(-1, width), w_rows.reshape(-1, w_out.shape[1])
    return [lax.all_gather(value, "heads", axis=0, tiled=True) for value in (tokens, w_out)]


def dense_experts(
    hidden_float, normed, w_gate, w_up, w_down, expert_ids, gate_weights, expert_count
):
    axes = ("ctx", "heads")
    exp_local = w_gate.shape[0]
    chosen = expert_ids[:, :, None] == jnp.arange(expert_count, dtype=jnp.int32)
    table = jnp.sum(jnp.where(chosen, gate_weights[:, :, None], 0.0), axis=1)
    first = lax.axis_index(axes) * exp_local
    rows, tables = gather_blocks(
        ("group", "group"), (normed, table.T), 0, "gather_rows"
    )
    device_count, row_count, width = rows.shape
    rows = rows.reshape(device_count * row_count, width)
    routed = 0.0
    for e in range(exp_local):
        gate_act = jnp.dot(rows, w_gate[e], preferred_element_type=jnp.float32)
        up_act = jnp.dot(rows, w_up[e], preferred_element_type=jnp.float32)
        hid = (jax.nn.silu(gate_act) * up_act).astype(jnp.bfloat16)
        weight = lax.dynamic_index_in_dim(tables, first + e, 1, False)
        weight = jnp.broadcast_to(weight[:, :, None], (device_count, row_count, HDIM))
        hid = hid.reshape(device_count, row_count, hid.shape[1])
        routed = routed + scatter_sums(hid, w_down[e], weight)
    return (hidden_float + routed).astype(jnp.bfloat16)


def on_device(
    tokens, state_in, past_kv, w_qkv, w_out, w_gate, w_up, w_down, expert_ids, gate_weights
):
    row_count, model_width = tokens.shape
    inner_width = w_qkv.shape[2]
    local_heads = inner_width // HDIM
    w_flat = w_qkv.reshape(model_width, 3 * inner_width)
    slab, w_rows = gather_inputs(tokens, w_out)
    projected = jnp.dot(
        slab,
        w_flat,
        preferred_element_type=jnp.float32,
    ).astype(jnp.bfloat16)
    slab_rows = projected.shape[0]
    projected = projected.reshape(slab_rows, 3, local_heads, HDIM)
    query = jnp.transpose(projected[:, 0], (1, 0, 2))
    keys = jnp.transpose(projected[:, 1], (1, 0, 2))
    values = jnp.transpose(projected[:, 2], (1, 0, 2))
    local_state = jnp.einsum("hsd,hse->hde", keys, values, preferred_element_type=jnp.float32)
    earlier_state = entering(
        local_state, "ctx", lambda first, second: first + second, jnp.zeros_like(local_state)
    )
    start_state = state_in + earlier_state
    tail = jnp.stack([keys, values], axis=0)
    arrived = from_behind(tail, "ctx", 1)
    past = jnp.transpose(past_kv.reshape(2, WINDOW, local_heads, HDIM), (0, 2, 1, 3))
    previous = jnp.where(lax.axis_index("ctx") == 0, past, arrived)
    all_keys = jnp.concatenate([previous[0], keys], axis=1)
    all_values = jnp.concatenate([previous[1], values], axis=1)
    block_rows = min(slab_rows, 512)
    block_count = slab_rows // block_rows
    scale = 1.0 / math.sqrt(HDIM)
    causal = jnp.arange(block_rows)[:, None] >= jnp.arange(block_rows)[None, :]
    offsets = jnp.arange(WINDOW + block_rows)[None, :] - jnp.arange(block_rows)[:, None]
    in_window = (offsets > 0) & (offsets <= WINDOW)

    def block_step(state, index):
        first = index * block_rows
        carried = jnp.einsum(
            "hsd,hde->hse", query.astype(jnp.float32), state, precision=lax.Precision.HIGHEST
        )
        inside = jnp.einsum("hsd,htd->hst", query, keys, preferred_element_type=jnp.float32)
        inside = jnp.where(causal[None], inside, 0.0).astype(jnp.bfloat16)
        linear = carried + jnp.einsum(
            "hst,hte->hse", inside, values, preferred_element_type=jnp.float32
        )
        scores = (
            jnp.einsum("hsd,htd->hst", query, all_keys, preferred_element_type=jnp.float32) * scale
        )
        scores = jnp.where(in_window[None], scores, -jnp.inf)
        top_score = jnp.max(scores, axis=-1, keepdims=True)
        expo = jnp.exp(scores - top_score)
        probs = (expo / jnp.sum(expo, axis=-1, keepdims=True)).astype(jnp.bfloat16)
        window_out = jnp.einsum(
            "hst,hte->hse", probs, all_values, preferred_element_type=jnp.float32
        )
        combined = (normalize(linear) + window_out).astype(jnp.bfloat16)
        new_state = state + jnp.einsum(
            "hsd,hse->hde", keys, values, preferred_element_type=jnp.float32
        )
        return (new_state, combined)

    _, outs = lax.scan(block_step, start_state, jnp.arange(block_count, dtype=jnp.int32))
    heads_out = jnp.transpose(outs, (0, 2, 1, 3)).reshape(slab_rows, inner_width)
    regrouped = lax.all_to_all(heads_out, "heads", split_axis=0, concat_axis=1, tiled=True)
    attn = jnp.dot(
        regrouped,
        w_rows,
        preferred_element_type=jnp.float32,
    )
    hidden_state = (tokens.astype(jnp.float32) + attn).astype(jnp.bfloat16)
    hidden_float = hidden_state.astype(jnp.float32)
    normed = normalize(hidden_float).astype(jnp.bfloat16)
    ctx_count = lax.axis_size("ctx")
    head_count = lax.axis_size("heads")
    exp_local = w_gate.shape[0]
    expert_count = exp_local * ctx_count * head_count
    top_count = expert_ids.shape[1]
    capacity = max(2, 2 * row_count * top_count // expert_count)
    devices = ctx_count * head_count
    if ctx_count == 4 and row_count * devices <= expert_count * capacity:
        return dense_experts(
            hidden_float, normed, w_gate, w_up, w_down, expert_ids, gate_weights, expert_count
        )
    picks = expert_ids.reshape(-1)
    onehot = (picks[:, None] == jnp.arange(expert_count, dtype=jnp.int32)[None, :]).astype(
        jnp.int32
    )
    earlier = jnp.cumsum(onehot, axis=0) - onehot
    slots = jnp.sum(onehot * earlier, axis=1)
    destination = picks * capacity + slots
    source_rows = jnp.arange(row_count * top_count, dtype=jnp.int32) // top_count
    outgoing = jnp.zeros((expert_count * capacity, model_width), jnp.bfloat16)
    outgoing = outgoing.at[destination].set(normed[source_rows])
    sendable = outgoing.reshape(expert_count, 1, capacity, model_width)
    arrived_rows = lax.all_to_all(
        sendable, ("ctx", "heads"), split_axis=0, concat_axis=1, tiled=True
    )
    e_count, n_count, c_count, d_count = arrived_rows.shape
    flat = arrived_rows.reshape(e_count, n_count * c_count, d_count)
    gate_act = jnp.einsum("erd,edf->erf", flat, w_gate, preferred_element_type=jnp.float32)
    up_act = jnp.einsum("erd,edf->erf", flat, w_up, preferred_element_type=jnp.float32)
    hid = (jax.nn.silu(gate_act) * up_act).astype(jnp.bfloat16)
    out_rows = jnp.einsum("erf,efd->erd", hid, w_down, preferred_element_type=jnp.float32)
    finished = out_rows.astype(jnp.bfloat16).reshape(e_count, n_count, c_count, d_count)
    returned = lax.all_to_all(finished, ("ctx", "heads"), split_axis=1, concat_axis=0, tiled=True)
    returned = returned.reshape(expert_count * capacity, model_width)
    picked = returned[destination].reshape(row_count, top_count, model_width).astype(jnp.float32)
    routed = jnp.sum(gate_weights[:, :, None] * picked, axis=1)
    return (hidden_float + routed).astype(jnp.bfloat16)


def solution(mesh):
    return jax.shard_map(
        on_device,
        mesh=mesh,
        in_specs=(
            P(("groups", "ctx", "heads"), None),
            P("heads", "groups", None),
            P(None, "groups", "heads"),
            P(None, None, "heads"),
            P("heads", None),
            P(("ctx", "heads"), None, None),
            P(("ctx", "heads"), None, None),
            P(("ctx", "heads"), None, None),
            P(("groups", "ctx", "heads"), None),
            P(("groups", "ctx", "heads"), None),
        ),
        out_specs=P(("groups", "ctx", "heads"), None),
        check_vma=False,
    )
```

```python
import functools
import math

import jax
import jax.numpy as jnp
from jax import lax
from jax.experimental import pallas as pl
from jax.experimental.pallas import tpu as pltpu
from jax.sharding import PartitionSpec as P

HDIM = 128
WINDOW = 512


def entering(x, axis, join, neutral):
    place = lax.axis_index(axis)
    gathered = lax.all_gather(x.astype(jnp.bfloat16), axis)
    state = jnp.zeros_like(x) + jnp.asarray(neutral, x.dtype)

    def one(lap, state):
        return join(state, lax.dynamic_index_in_dim(gathered, lap, 0, False).astype(x.dtype))

    return lax.fori_loop(0, place, one, state)


def from_behind(block, axis, distance):
    devices = range(lax.axis_size(axis))
    route = [(i - distance, i) for i in devices if i - distance in devices]
    return lax.ppermute(block, axis, route)


def normalize(value):
    return value * lax.rsqrt(jnp.mean(value * value, axis=-1, keepdims=True) + 1e-06)


MESH = pl.DeviceIdType.MESH
VMEM_BYTES = 60 * 1024 * 1024
ADD_ROWS = 16
DOT_COLUMNS = 512
LAG = 2


def place(count):
    z = lax.axis_index("heads")
    c = lax.axis_index("ctx")
    beside = c + 1 - 2 * lax.rem(c, 2)
    across = lax.rem(c + 2, 4)
    diagonal = lax.rem(beside + 2, 4)
    return z, c, beside, across, diagonal


def greet(z, count, beside, across):
    barrier = pltpu.get_barrier_semaphore()

    def signal(target):
        pl.semaphore_signal(barrier, inc=1, device_id=target, device_id_type=MESH)

    signal({"ctx": beside})
    signal({"ctx": across})

    @pl.when(z > 0)
    def _():
        signal({"heads": z - 1})

    @pl.when(z < count - 1)
    def _():
        signal({"heads": z + 1})

    pl.semaphore_wait(barrier, 2 + jnp.minimum(z, 1) + jnp.minimum(count - 1 - z, 1))


def gather_kernel(count, kinds, *refs):
    size = len(kinds)
    groups = [refs[first * size : (first + 1) * size] for first in range(4)]
    own_sem = refs[4 * size]
    z, c, beside, across, diagonal = place(count)
    greet(z, count, beside, across)

    def origin(kind, source, full):
        if kind != "share":
            return source
        share = full.shape[1]
        return source.at[pl.ds(pl.multiple_of(c * share, share), share), :]

    def slot_of(kind, zz, cc):
        return {"group": cc * count + zz, "share": zz * 4 + cc, "line": zz}[kind]

    def copies(zz, cc, way, target, own=False):
        result = []
        for kind, source, full, send, recv in zip(kinds, *groups):
            if kind == "line" and (way > 1 or cc is not c):
                continue
            slot = slot_of(kind, zz, cc)
            result.append(
                pltpu.make_async_remote_copy(
                    src_ref=origin(kind, source, full) if own else full.at[slot],
                    dst_ref=full.at[slot],
                    send_sem=send.at[way, slot],
                    recv_sem=recv.at[slot],
                    device_id=target,
                    device_id_type=MESH,
                )
            )
        return result

    def start(zz, cc, way, target, own=False):
        for copy in copies(zz, cc, way, target, own):
            copy.start()

    def arrived(zz, cc):
        for copy in copies(zz, cc, 0, {"ctx": beside}):
            copy.wait_recv()

    def left(zz, cc, way, target):
        for copy in copies(zz, cc, way, target):
            copy.wait_send()

    def along(act, down, up, zz, **options):
        if down:

            @pl.when(z > 0)
            def _():
                act(zz, c, 0, {"heads": z - 1}, **options)

        if up:

            @pl.when(z < count - 1)
            def _():
                act(zz, c, 1, {"heads": z + 1}, **options)

        act(zz, c, 2, {"ctx": across}, **options)
        act(zz, c, 3, {"ctx": beside}, **options)

    local = [
        pltpu.make_async_copy(
            origin(kind, source, full), full.at[slot_of(kind, z, c)], own_sem.at[index]
        )
        for index, (kind, source, full) in enumerate(zip(kinds, *groups[:2]))
    ]
    for copy in local:
        copy.start()
    along(start, True, True, z, own=True)

    def over(zz):
        arrived(zz, across)
        start(zz, across, 3, {"ctx": beside})

    for d in range(1, count + 1):
        if d < count:

            @pl.when(z >= d)
            def _():
                arrived(z - d, c)
                along(start, False, True, z - d)

            @pl.when(z + d < count)
            def _():
                arrived(z + d, c)
                along(start, True, False, z + d)

        if d == 1:
            over(z)
        else:

            @pl.when(z >= d - 1)
            def _():
                over(z - d + 1)

            @pl.when(z + d - 1 < count)
            def _():
                over(z + d - 1)

    for zz in range(count):
        arrived(zz, beside)
        arrived(zz, diagonal)
    for copy in local:
        copy.wait()
    along(left, True, True, z)
    for d in range(1, count):

        @pl.when(z >= d)
        def _():
            along(left, False, True, z - d)

        @pl.when(z + d < count)
        def _():
            along(left, True, False, z + d)

    for zz in range(count):
        left(zz, across, 3, {"ctx": beside})


def scatter_kernel(
    count, hid_ref, down_ref, weight_ref, out_ref, part_ref, from_beside, from_across, below, above, to_across, to_line,
    beside_send, beside_recv, across_send, across_recv, line_send, below_recv, above_recv,
):
    z, c, beside, across, diagonal = place(count)
    greet(z, count, beside, across)

    def nth(index):
        more = jnp.maximum(z, count - 1 - z)
        fewer = count - 1 - more
        alone = more - fewer
        paired = jnp.maximum(index - alone, 0)
        up = jnp.where(z + more < count, more - index, index - more)
        both = (fewer - paired // 2) * (1 - 2 * (paired % 2))
        offset = jnp.where(index < alone, up, both)
        return z + jnp.where(index < count - 1, offset, 0)

    def compute(slot):
        weight = weight_ref[slot][:, :1]

        def tile(index, _):
            columns = pl.ds(pl.multiple_of(index * DOT_COLUMNS, DOT_COLUMNS), DOT_COLUMNS)
            product = jnp.dot(
                hid_ref[slot], down_ref[:, columns], preferred_element_type=jnp.float32
            )
            part_ref[slot, :, columns] = (weight * product).astype(part_ref.dtype)
            return 0

        lax.fori_loop(0, down_ref.shape[1] // DOT_COLUMNS, tile, 0)

    def beside_copy(kind, zz):
        cc = diagonal if kind == 0 else beside
        return pltpu.make_async_remote_copy(
            src_ref=part_ref.at[cc * count + zz],
            dst_ref=from_beside.at[kind, zz],
            send_sem=beside_send.at[kind, zz],
            recv_sem=beside_recv.at[kind, zz],
            device_id={"ctx": beside},
            device_id_type=MESH,
        )

    def across_copy(zz):
        return pltpu.make_async_remote_copy(
            src_ref=to_across.at[zz],
            dst_ref=from_across.at[zz],
            send_sem=across_send.at[zz],
            recv_sem=across_recv.at[zz],
            device_id={"ctx": across},
            device_id_type=MESH,
        )

    def up_copy(zz):
        return pltpu.make_async_remote_copy(
            src_ref=to_line.at[zz],
            dst_ref=below.at[zz],
            send_sem=line_send.at[zz],
            recv_sem=below_recv.at[zz],
            device_id={"heads": z + 1},
            device_id_type=MESH,
        )

    def down_copy(zz):
        return pltpu.make_async_remote_copy(
            src_ref=to_line.at[zz],
            dst_ref=above.at[zz],
            send_sem=line_send.at[zz],
            recv_sem=above_recv.at[zz],
            device_id={"heads": z - 1},
            device_id_type=MESH,
        )

    def add(target, sources):
        def chunk(index, _):
            rows = pl.ds(pl.multiple_of(index * ADD_ROWS, ADD_ROWS), ADD_ROWS)
            total = sources[0][rows, :].astype(jnp.float32)
            for source in sources[1:]:
                total = total + source[rows, :].astype(jnp.float32)
            target[rows, :] = total.astype(target.dtype)
            return 0

        lax.fori_loop(0, target.shape[0] // ADD_ROWS, chunk, 0)

    def project(zz):
        compute(diagonal * count + zz)
        beside_copy(0, zz).start()
        compute(across * count + zz)
        beside_copy(0, zz).wait_recv()
        add(to_across.at[zz], [part_ref.at[across * count + zz], from_beside.at[0, zz]])
        across_copy(zz).start()
        compute(beside * count + zz)
        beside_copy(1, zz).start()
        compute(c * count + zz)

    def onward(zz, copy, arriving, first, sources):
        @pl.when(first)
        def _():
            add(to_line.at[zz], sources)

        @pl.when(jnp.logical_not(first))
        def _():
            copy(zz).wait_recv()
            add(to_line.at[zz], sources + [arriving.at[zz]])

        copy(zz).start()

    def pass_line(zz):
        beside_copy(1, zz).wait_recv()
        across_copy(zz).wait_recv()
        sources = [part_ref.at[c * count + zz], from_beside.at[1, zz], from_across.at[zz]]

        @pl.when(zz > z)
        def _():
            onward(zz, up_copy, below, z == 0, sources)

        @pl.when(zz < z)
        def _():
            onward(zz, down_copy, above, z == count - 1, sources)

        @pl.when(zz == z)
        def _():
            add(out_ref, sources)

            @pl.when(z > 0)
            def _():
                up_copy(zz).wait_recv()
                add(out_ref, [out_ref, below.at[zz]])

            @pl.when(z < count - 1)
            def _():
                down_copy(zz).wait_recv()
                add(out_ref, [out_ref, above.at[zz]])

    def step(index, _):
        @pl.when(index < count)
        def _():
            project(nth(index))

        @pl.when(index >= LAG)
        def _():
            pass_line(nth(index - LAG))

        return 0

    lax.fori_loop(0, count + LAG, step, 0)

    for zz in range(count):
        beside_copy(0, zz).wait_send()
        beside_copy(1, zz).wait_send()
        across_copy(zz).wait_send()

        @pl.when(zz > z)
        def _():
            up_copy(zz).wait_send()

        @pl.when(zz < z)
        def _():
            down_copy(zz).wait_send()


def gather_blocks(kinds, operands, collective_id, name):
    count, ctx_count = lax.axis_size("heads"), lax.axis_size("ctx")
    slots = [count if kind == "line" else count * ctx_count for kind in kinds]
    shapes = [
        (value.shape[0] // ctx_count if kind == "share" else value.shape[0], value.shape[1])
        for kind, value in zip(kinds, operands)
    ]
    return pl.pallas_call(
        functools.partial(gather_kernel, count, kinds),
        out_shape=[
            jax.ShapeDtypeStruct((slot,) + shape, value.dtype)
            for slot, shape, value in zip(slots, shapes, operands)
        ],
        in_specs=[pl.BlockSpec(memory_space=pltpu.VMEM)] * len(kinds),
        out_specs=[pl.BlockSpec(memory_space=pltpu.VMEM)] * len(kinds),
        scratch_shapes=[pltpu.SemaphoreType.DMA((4, slot)) for slot in slots]
        + [pltpu.SemaphoreType.DMA((slot,)) for slot in slots]
        + [pltpu.SemaphoreType.DMA((len(kinds),))],
        compiler_params=pltpu.CompilerParams(
            collective_id=collective_id, has_side_effects=True, vmem_limit_bytes=VMEM_BYTES
        ),
        name=name,
    )(*operands)


def scatter_sums(hid, down, weights):
    count = lax.axis_size("heads")
    devices, rows, _ = hid.shape
    block = (rows, down.shape[1])
    dma = pltpu.SemaphoreType.DMA
    return pl.pallas_call(
        functools.partial(scatter_kernel, count),
        out_shape=jax.ShapeDtypeStruct(block, jnp.float32),
        in_specs=[pl.BlockSpec(memory_space=pltpu.VMEM)] * 3,
        out_specs=pl.BlockSpec(memory_space=pltpu.VMEM),
        scratch_shapes=[
            pltpu.VMEM((devices,) + block, hid.dtype),
            pltpu.VMEM((2, count) + block, hid.dtype),
        ]
        + [pltpu.VMEM((count,) + block, hid.dtype)] * 5
        + [dma((2, count))] * 2
        + [dma((count,))] * 5,
        compiler_params=pltpu.CompilerParams(
            collective_id=1, has_side_effects=True, vmem_limit_bytes=VMEM_BYTES
        ),
        name="scatter_sums",
    )(hid, down, weights)


def gather_inputs(tokens, w_out):
    if lax.axis_size("ctx") == 4 and w_out.shape[0] % 64 == 0:
        slab, w_rows = gather_blocks(("line", "share"), (tokens, w_out), 2, "gather_inputs")
        width = tokens.shape[1]
        return slab.reshape(-1, width), w_rows.reshape(-1, w_out.shape[1])
    return [lax.all_gather(value, "heads", axis=0, tiled=True) for value in (tokens, w_out)]


def dense_experts(
    hidden_float, normed, w_gate, w_up, w_down, expert_ids, gate_weights, expert_count
):
    axes = ("ctx", "heads")
    exp_local = w_gate.shape[0]
    chosen = expert_ids[:, :, None] == jnp.arange(expert_count, dtype=jnp.int32)
    table = jnp.sum(jnp.where(chosen, gate_weights[:, :, None], 0.0), axis=1)
    first = lax.axis_index(axes) * exp_local
    rows, tables = gather_blocks(
        ("group", "group"), (normed, table.T), 0, "gather_rows"
    )
    device_count, row_count, width = rows.shape
    rows = rows.reshape(device_count * row_count, width)
    routed = 0.0
    for e in range(exp_local):
        gate_act = jnp.dot(rows, w_gate[e], preferred_element_type=jnp.float32)
        up_act = jnp.dot(rows, w_up[e], preferred_element_type=jnp.float32)
        hid = (jax.nn.silu(gate_act) * up_act).astype(jnp.bfloat16)
        weight = lax.dynamic_index_in_dim(tables, first + e, 1, False)
        weight = jnp.broadcast_to(weight[:, :, None], (device_count, row_count, HDIM))
        hid = hid.reshape(device_count, row_count, hid.shape[1])
        routed = routed + scatter_sums(hid, w_down[e], weight)
    return (hidden_float + routed).astype(jnp.bfloat16)


def on_device(
    tokens, state_in, past_kv, w_qkv, w_out, w_gate, w_up, w_down, expert_ids, gate_weights
):
    row_count, model_width = tokens.shape
    inner_width = w_qkv.shape[2]
    local_heads = inner_width // HDIM
    w_flat = w_qkv.reshape(model_width, 3 * inner_width)
    slab, w_rows = gather_inputs(tokens, w_out)
    projected = jnp.dot(
        slab,
        w_flat,
        preferred_element_type=jnp.float32,
    ).astype(jnp.bfloat16)
    slab_rows = projected.shape[0]
    projected = projected.reshape(slab_rows, 3, local_heads, HDIM)
    query = jnp.transpose(projected[:, 0], (1, 0, 2))
    keys = jnp.transpose(projected[:, 1], (1, 0, 2))
    values = jnp.transpose(projected[:, 2], (1, 0, 2))
    local_state = jnp.einsum("hsd,hse->hde", keys, values, preferred_element_type=jnp.float32)
    earlier_state = entering(
        local_state, "ctx", lambda first, second: first + second, jnp.zeros_like(local_state)
    )
    start_state = state_in + earlier_state
    tail = jnp.stack([keys, values], axis=0)
    arrived = from_behind(tail, "ctx", 1)
    past = jnp.transpose(past_kv.reshape(2, WINDOW, local_heads, HDIM), (0, 2, 1, 3))
    previous = jnp.where(lax.axis_index("ctx") == 0, past, arrived)
    all_keys = jnp.concatenate([previous[0], keys], axis=1)
    all_values = jnp.concatenate([previous[1], values], axis=1)
    block_rows = min(slab_rows, 512)
    block_count = slab_rows // block_rows
    scale = 1.0 / math.sqrt(HDIM)
    causal = jnp.arange(block_rows)[:, None] >= jnp.arange(block_rows)[None, :]
    offsets = jnp.arange(WINDOW + block_rows)[None, :] - jnp.arange(block_rows)[:, None]
    in_window = (offsets > 0) & (offsets <= WINDOW)

    def block_step(state, index):
        first = index * block_rows
        carried = jnp.einsum(
            "hsd,hde->hse", query.astype(jnp.float32), state, precision=lax.Precision.HIGHEST
        )
        inside = jnp.einsum("hsd,htd->hst", query, keys, preferred_element_type=jnp.float32)
        inside = jnp.where(causal[None], inside, 0.0).astype(jnp.bfloat16)
        linear = carried + jnp.einsum(
            "hst,hte->hse", inside, values, preferred_element_type=jnp.float32
        )
        scores = (
            jnp.einsum("hsd,htd->hst", query, all_keys, preferred_element_type=jnp.float32) * scale
        )
        scores = jnp.where(in_window[None], scores, -jnp.inf)
        top_score = jnp.max(scores, axis=-1, keepdims=True)
        expo = jnp.exp(scores - top_score)
        probs = (expo / jnp.sum(expo, axis=-1, keepdims=True)).astype(jnp.bfloat16)
        window_out = jnp.einsum(
            "hst,hte->hse", probs, all_values, preferred_element_type=jnp.float32
        )
        combined = (normalize(linear) + window_out).astype(jnp.bfloat16)
        new_state = state + jnp.einsum(
            "hsd,hse->hde", keys, values, preferred_element_type=jnp.float32
        )
        return (new_state, combined)

    _, outs = lax.scan(block_step, start_state, jnp.arange(block_count, dtype=jnp.int32))
    heads_out = jnp.transpose(outs, (0, 2, 1, 3)).reshape(slab_rows, inner_width)
    regrouped = lax.all_to_all(heads_out, "heads", split_axis=0, concat_axis=1, tiled=True)
    attn = jnp.dot(
        regrouped,
        w_rows,
        preferred_element_type=jnp.float32,
    )
    hidden_state = (tokens.astype(jnp.float32) + attn).astype(jnp.bfloat16)
    hidden_float = hidden_state.astype(jnp.float32)
    normed = normalize(hidden_float).astype(jnp.bfloat16)
    ctx_count = lax.axis_size("ctx")
    head_count = lax.axis_size("heads")
    exp_local = w_gate.shape[0]
    expert_count = exp_local * ctx_count * head_count
    top_count = expert_ids.shape[1]
    capacity = max(2, 2 * row_count * top_count // expert_count)
    devices = ctx_count * head_count
    if ctx_count == 4 and row_count * devices <= expert_count * capacity:
        return dense_experts(
            hidden_float, normed, w_gate, w_up, w_down, expert_ids, gate_weights, expert_count
        )
    picks = expert_ids.reshape(-1)
    onehot = (picks[:, None] == jnp.arange(expert_count, dtype=jnp.int32)[None, :]).astype(
        jnp.int32
    )
    earlier = jnp.cumsum(onehot, axis=0) - onehot
    slots = jnp.sum(onehot * earlier, axis=1)
    destination = picks * capacity + slots
    source_rows = jnp.arange(row_count * top_count, dtype=jnp.int32) // top_count
    outgoing = jnp.zeros((expert_count * capacity, model_width), jnp.bfloat16)
    outgoing = outgoing.at[destination].set(normed[source_rows])
    sendable = outgoing.reshape(expert_count, 1, capacity, model_width)
    arrived_rows = lax.all_to_all(
        sendable, ("ctx", "heads"), split_axis=0, concat_axis=1, tiled=True
    )
    e_count, n_count, c_count, d_count = arrived_rows.shape
    flat = arrived_rows.reshape(e_count, n_count * c_count, d_count)
    gate_act = jnp.einsum("erd,edf->erf", flat, w_gate, preferred_element_type=jnp.float32)
    up_act = jnp.einsum("erd,edf->erf", flat, w_up, preferred_element_type=jnp.float32)
    hid = (jax.nn.silu(gate_act) * up_act).astype(jnp.bfloat16)
    out_rows = jnp.einsum("erf,efd->erd", hid, w_down, preferred_element_type=jnp.float32)
    finished = out_rows.astype(jnp.bfloat16).reshape(e_count, n_count, c_count, d_count)
    returned = lax.all_to_all(finished, ("ctx", "heads"), split_axis=1, concat_axis=0, tiled=True)
    returned = returned.reshape(expert_count * capacity, model_width)
    picked = returned[destination].reshape(row_count, top_count, model_width).astype(jnp.float32)
    routed = jnp.sum(gate_weights[:, :, None] * picked, axis=1)
    return (hidden_float + routed).astype(jnp.bfloat16)


def solution(mesh):
    return jax.shard_map(
        on_device,
        mesh=mesh,
        in_specs=(
            P(("groups", "ctx", "heads"), None),
            P("heads", "groups", None),
            P(None, "groups", "heads"),
            P(None, None, "heads"),
            P("heads", None),
            P(("ctx", "heads"), None, None),
            P(("ctx", "heads"), None, None),
            P(("ctx", "heads"), None, None),
            P(("groups", "ctx", "heads"), None),
            P(("groups", "ctx", "heads"), None),
        ),
        out_specs=P(("groups", "ctx", "heads"), None),
        check_vma=False,
    )
```
